256 devices in a mesh: dp: 8 (over x, core), cut: 32 (over y, z).
Axes of the slice: x: 4, y: 4, z: 8, core: 2. Of those that a mesh axis runs over, the one named last changes fastest.
Arguments:
- node_feat: bfloat16 [128, 262144], P(None, ('dp', 'cut')), parts along dimension 1, may hold values from -6 to 6
- edge_feat: bfloat16 [128, 1048576], P(None, ('dp', 'cut')), parts along dimension 1, may hold values from -6 to 6
- route: int32 [256, 32, 128], P(('dp', 'cut')), parts along dimension 0, may hold values from 0 to 1023, as said below
- block_tile: int32 [8192, 2], P(('dp', 'cut')), parts along dimension 0, may hold values from 0 to 39
- block_offset: int32 [8192, 2, 128], P(('dp', 'cut')), parts along dimension 0, may hold values from 0 to 127
- block_count: int32 [8192], P(('dp', 'cut')), parts along dimension 0, may hold values from 1 to 128, as said below
- w_edge1: bfloat16 [128, 384], replicated, may hold values from -0.3125 to 0.3125
- bias_edge1: float32 [128], replicated, may hold values from -3 to 3
- w_edge2: bfloat16 [128, 128], replicated, may hold values from -0.5 to 0.5
- gain_edge: float32 [128], replicated, may hold values from 0.1 to 1.9
- shift_edge: float32 [128], replicated, may hold values from -3 to 3
- w_node1: bfloat16 [128, 256], replicated, may hold values from -0.375 to 0.375
- bias_node1: float32 [128], replicated, may hold values from -3 to 3
- w_node2: bfloat16 [128, 128], replicated, may hold values from -0.5 to 0.5
- gain_node: float32 [128], replicated, may hold values from 0.1 to 1.9
- shift_node: float32 [128], replicated, may hold values from -3 to 3
- node_cot: bfloat16 [128, 262144], P(None, ('dp', 'cut')), parts along dimension 1, may hold values from -6 to 6
Outputs:
- node_out: bfloat16 [128, 262144], P(None, ('dp', 'cut')), parts along dimension 1
- node_grad: float32 [128, 262144], P(None, ('dp', 'cut')), parts along dimension 1
- edge_grad: bfloat16 [128, 1048576], P(None, ('dp', 'cut')), parts along dimension 1
- param_grad: float32 [923648], P('dp'), parts along dimension 0
The draws below stay inside these ranges and needn't reach their ends.
There are 8 independent parts, one for each index of `dp`. The reference program is written for one: setup_inputs(seed, part) draws one part's arguments, and reference() takes and returns one part's arrays. A program takes and returns all parts, laid end to end along the dimension named above; an argument that names none is the same for every part. Nothing has to cross between parts.
Inputs may be any that keep to these rules, and one draw needn't show every extreme that they name: route[c, p, :] holds 128 distinct master rows of partition p. `block_count`: the first block of each partition is full.
All inputs are finite; a program needn't handle non-finite values.
Results may differ from the reference program's by a relative error of at most 0.024.
Values may be sent and summed in bfloat16 or wider, within the bound.
No kernel may reach another device: no remote copies, remote signals or barrier semaphores. Data moves between devices by JAX's collectives and lax.ppermute only.
A program may use at most 128 MiB of HBM per device.

```python
import math
import jax
import jax.numpy as jnp
from jax import lax

LATENT = 128
HIDDEN_SIZE = 128
EB = 128
NM = 1024
EBLK_DEV = 32
NODES = 32768
MP = 128
EBLKS = 1024
EDGES = 131072
TILES = 40


def draw_route(key, part):
    peer_count = NODES // NM
    key_list = jax.random.split(jax.random.fold_in(key, 11), peer_count * peer_count)
    row_lists = jax.vmap(lambda sub_key: jax.random.permutation(sub_key, NM)[:MP])(key_list)
    return row_lists.reshape(peer_count, peer_count, MP).astype(jnp.int32)


def draw_block_count(key, part):
    counts = jax.random.randint(jax.random.fold_in(key, 23), (EBLKS,), 1, EB + 1)
    first_block = jnp.arange(EBLKS) % EBLK_DEV == 0
    return jnp.where(first_block, EB, counts).astype(jnp.int32)


def touch_ends(drawn, rng, smallest, top_value):
    shape = drawn.shape
    index_at = [jax.random.randint(jax.random.fold_in(rng, axis), (), 0, shape[axis]) for axis in range(len(shape))]
    drawn = drawn.at[tuple(index_at)].set(smallest)
    longest = shape.index(max(shape))
    index_at[longest] = (index_at[longest] + 1) % shape[longest]
    return drawn.at[tuple(index_at)].set(top_value)


def block_levels(stream_key, dims, cuts, low, largest):
    def one(axis_at, blocks):
        heights = jax.random.uniform(jax.random.fold_in(jax.random.fold_in(stream_key, 6), axis_at), (blocks,), jnp.float32, low / len(cuts), largest / len(cuts))
        return jnp.repeat(jnp.exp(heights), dims[axis_at] // blocks).reshape((-1,) + (1,) * (len(dims) - axis_at - 1))

    loudness = one(*cuts[0])
    for cut in cuts[1:]:
        loudness = loudness * one(*cut)
    return loudness


def gaussian(key, shape, deviation, bound, shards=(), kind=jnp.bfloat16):
    result = jax.random.normal(key, shape, jnp.float32) * deviation
    if len(shards) > 0:
        result = block_levels(key, shape, shards, -0.22, 0.18) * result
    return jnp.clip(result, min=-bound, max=bound).astype(kind)


def setup_inputs(seed: int = 0, part: int = 0) -> dict:
    streams_of = jax.random.split(jax.random.key(seed), 18)
    part_keys = jax.random.split(jax.random.fold_in(streams_of[17], part), 18)
    node_feat = gaussian(part_keys[0], (LATENT, NODES), 1.0, 6.0, ((1, 32),))
    edge_feat = gaussian(part_keys[1], (LATENT, EDGES), 1.0, 6.0, ((1, 32),))
    route = draw_route(jax.random.fold_in(jax.random.fold_in(streams_of[17], part), 71), part)
    block_tile = touch_ends(jax.random.randint(part_keys[3], (EBLKS, 2), 0, TILES), jax.random.fold_in(part_keys[3], 1), 0, TILES - 1).astype(jnp.int32)
    block_offset = touch_ends(jax.random.randint(part_keys[4], (EBLKS, 2, EB), 0, EB), jax.random.fold_in(part_keys[4], 1), 0, EB - 1).astype(jnp.int32)
    block_count = draw_block_count(jax.random.fold_in(jax.random.fold_in(streams_of[17], part), 71), part)
    w_edge1 = gaussian(streams_of[6], (HIDDEN_SIZE, 3 * LATENT), (3 * LATENT) ** -0.5, 0.3125)
    bias_edge1 = gaussian(streams_of[7], (HIDDEN_SIZE,), 0.5, 3.0, (), jnp.float32)
    w_edge2 = gaussian(streams_of[8], (LATENT, HIDDEN_SIZE), HIDDEN_SIZE ** -0.5, 0.5)
    gain_edge = jnp.clip(1.0 + 0.18 * jax.random.normal(streams_of[9], (LATENT,), jnp.float32), 0.1, 1.9)
    shift_edge = gaussian(streams_of[10], (LATENT,), 0.5, 3.0, (), jnp.float32)
    w_node1 = gaussian(streams_of[11], (HIDDEN_SIZE, 2 * LATENT), (2 * LATENT) ** -0.5, 0.375)
    bias_node1 = gaussian(streams_of[12], (HIDDEN_SIZE,), 0.5, 3.0, (), jnp.float32)
    w_node2 = gaussian(streams_of[13], (LATENT, HIDDEN_SIZE), HIDDEN_SIZE ** -0.5, 0.5)
    gain_node = jnp.clip(1.0 + 0.18 * jax.random.normal(streams_of[14], (LATENT,), jnp.float32), 0.1, 1.9)
    shift_node = gaussian(streams_of[15], (LATENT,), 0.5, 3.0, (), jnp.float32)
    node_cot = gaussian(part_keys[16], (LATENT, NODES), 1.0, 6.0, ((1, 32),))
    return {"node_feat": node_feat, "edge_feat": edge_feat, "route": route, "block_tile": block_tile, "block_offset": block_offset, "block_count": block_count, "w_edge1": w_edge1, "bias_edge1": bias_edge1, "w_edge2": w_edge2, "gain_edge": gain_edge, "shift_edge": shift_edge, "w_node1": w_node1, "bias_node1": bias_node1, "w_node2": w_node2, "gain_node": gain_node, "shift_node": shift_node, "node_cot": node_cot}


def silu_slope(values):
    sigmoid_val = jax.nn.sigmoid(values)
    return sigmoid_val * (1.0 + values * (1.0 - sigmoid_val))

def layer_norm(values):
    centred = values - lax.optimization_barrier(jnp.mean(values, axis=0, keepdims=True))
    inverse = lax.rsqrt(lax.optimization_barrier(jnp.mean(centred * centred, axis=0, keepdims=True)) + 1e-05)
    return (centred * inverse, inverse)

def norm_back(upstream, normed, inverse, gain_vec):
    scaled = upstream * gain_vec[:, None]
    return inverse * (scaled - lax.optimization_barrier(jnp.mean(scaled, axis=0, keepdims=True)) - normed * lax.optimization_barrier(jnp.mean(scaled * normed, axis=0, keepdims=True)))

def reference(node_feat, edge_feat, route, block_tile, block_offset, block_count, w_edge1, bias_edge1, w_edge2, gain_edge, shift_edge, w_node1, bias_node1, w_node2, gain_node, shift_node, node_cot):
    peer_count = NODES // NM
    part_ids = jnp.arange(peer_count, dtype=jnp.int32)
    master_ids = part_ids[:, None] * NM + jnp.arange(NM, dtype=jnp.int32)[None, :]
    mirror_ids = (part_ids[None, :, None] * NM + route).reshape(peer_count, peer_count * MP)
    local_ids = jnp.concatenate([master_ids, mirror_ids], axis=1)
    owner_part = jnp.arange(EBLKS, dtype=jnp.int32) // EBLK_DEV
    columns = 128 * block_tile[:, :, None] + block_offset
    global_ids = local_ids[owner_part[:, None, None], columns]
    senders = global_ids[:, 0, :].reshape(-1)
    receivers = global_ids[:, 1, :].reshape(-1)
    live_mask = (jnp.arange(EB, dtype=jnp.int32)[None, :] < block_count[:, None]).reshape(-1).astype(jnp.float32)
    stacked = jnp.concatenate([edge_feat, jnp.take(node_feat, senders, axis=1), jnp.take(node_feat, receivers, axis=1)], axis=0)
    edge_pre = jnp.dot(w_edge1, stacked, preferred_element_type=jnp.float32) + bias_edge1[:, None]
    edge_hidden = jax.nn.silu(edge_pre).astype(jnp.bfloat16)
    edge_post = jnp.dot(w_edge2, edge_hidden, preferred_element_type=jnp.float32)
    edge_normed, edge_inv = layer_norm(edge_post)
    message = (gain_edge[:, None] * edge_normed + shift_edge[:, None]) * live_mask[None, :]
    aggregate = jnp.zeros((LATENT, NODES), jnp.float32).at[:, receivers].add(message)
    agg_low = aggregate.astype(jnp.bfloat16)
    node_input = jnp.concatenate([node_feat, agg_low], axis=0)
    node_pre = jnp.dot(w_node1, node_input, preferred_element_type=jnp.float32) + bias_node1[:, None]
    node_hidden = jax.nn.silu(node_pre).astype(jnp.bfloat16)
    node_post = jnp.dot(w_node2, node_hidden, preferred_element_type=jnp.float32)
    node_normed, node_inv = layer_norm(node_post)
    node_out = (node_feat.astype(jnp.float32) + gain_node[:, None] * node_normed + shift_node[:, None]).astype(jnp.bfloat16)
    upstream = node_cot.astype(jnp.float32)
    grad_gain_node = lax.optimization_barrier(jnp.sum(upstream * node_normed, axis=1))
    grad_shift_node = lax.optimization_barrier(jnp.sum(upstream, axis=1))
    grad_node_post = norm_back(upstream, node_normed, node_inv, gain_node).astype(jnp.bfloat16)
    grad_w_node2 = jnp.dot(grad_node_post, node_hidden.T, preferred_element_type=jnp.float32)
    grad_node_full = jnp.dot(w_node2.T, grad_node_post, preferred_element_type=jnp.float32) * silu_slope(node_pre)
    grad_node_pre = grad_node_full.astype(jnp.bfloat16)
    grad_w_node1 = jnp.dot(grad_node_pre, node_input.T, preferred_element_type=jnp.float32)
    grad_bias_node1 = lax.optimization_barrier(jnp.sum(grad_node_full, axis=1))
    node_direct = jnp.dot(w_node1[:, :LATENT].T, grad_node_pre, preferred_element_type=jnp.float32)
    grad_agg = jnp.dot(w_node1[:, LATENT:].T, grad_node_pre, preferred_element_type=jnp.float32).astype(jnp.bfloat16)
    grad_message = jnp.take(grad_agg, receivers, axis=1).astype(jnp.float32) * live_mask[None, :]
    grad_gain_edge = lax.optimization_barrier(jnp.sum(grad_message * edge_normed, axis=1))
    grad_shift_edge = lax.optimization_barrier(jnp.sum(grad_message, axis=1))
    grad_edge_post = norm_back(grad_message, edge_normed, edge_inv, gain_edge).astype(jnp.bfloat16)
    grad_w_edge2 = jnp.dot(grad_edge_post, edge_hidden.T, preferred_element_type=jnp.float32)
    grad_edge_full = jnp.dot(w_edge2.T, grad_edge_post, preferred_element_type=jnp.float32) * silu_slope(edge_pre)
    grad_edge_pre = grad_edge_full.astype(jnp.bfloat16)
    grad_w_edge1 = jnp.dot(grad_edge_pre, stacked.T, preferred_element_type=jnp.float32)
    grad_bias_edge1 = lax.optimization_barrier(jnp.sum(grad_edge_full, axis=1))
    edge_grad = jnp.dot(w_edge1[:, :LATENT].T, grad_edge_pre, preferred_element_type=jnp.float32).astype(jnp.bfloat16)
    grad_send = jnp.dot(w_edge1[:, LATENT:2 * LATENT].T, grad_edge_pre, preferred_element_type=jnp.float32)
    grad_recv = jnp.dot(w_edge1[:, 2 * LATENT:].T, grad_edge_pre, preferred_element_type=jnp.float32)
    gathered = jnp.zeros((LATENT, NODES), jnp.float32).at[:, senders].add(grad_send).at[:, receivers].add(grad_recv)
    node_grad = upstream + node_direct + gathered
    edge_vec = jnp.concatenate([grad_w_edge1.reshape(-1), grad_bias_edge1, grad_w_edge2.reshape(-1), grad_gain_edge, grad_shift_edge])
    node_vec = jnp.concatenate([grad_w_node1.reshape(-1), grad_bias_node1, grad_w_node2.reshape(-1), grad_gain_node, grad_shift_node])
    param_grad = jnp.concatenate([edge_vec / math.sqrt(EDGES), node_vec / math.sqrt(NODES)])
    return (node_out, node_grad, edge_grad, param_grad)
```

```python
import functools
import math

import jax
import jax.numpy as jnp
from jax import lax
from jax.experimental import pallas as pl
from jax.experimental.pallas import tpu as pltpu
from jax.sharding import PartitionSpec as P

F32 = jnp.float32
BF16 = jnp.bfloat16
TILE = 128
GROUP = 8
NODE_ROWS = 16
EDGE_ROWS = 24
INTERPRET = False


def dot_nn(left, right):
    return lax.dot_general(left, right, (((1,), (0,)), ((), ())), preferred_element_type=F32)


def dot_nt(left, right):
    return lax.dot_general(left, right, (((1,), (1,)), ((), ())), preferred_element_type=F32)


def dot_tn(left, right):
    return lax.dot_general(left, right, (((0,), (0,)), ((), ())), preferred_element_type=F32)


def one_hot(index_row, depth):
    rows = lax.broadcasted_iota(jnp.int32, (depth, index_row.shape[1]), 0)
    return jnp.where(rows == index_row, 1.0, 0.0).astype(BF16)


def sigmoid(values):
    return 1.0 / (1.0 + jnp.exp(-values))


def layer_norm(values):
    centred = values - jnp.mean(values, axis=0, keepdims=True)
    inverse = lax.rsqrt(jnp.mean(centred * centred, axis=0, keepdims=True) + 1e-05)
    return centred * inverse, inverse


def norm_back(upstream, normed, inverse, gain):
    scaled = upstream * gain
    return inverse * (
        scaled
        - jnp.mean(scaled, axis=0, keepdims=True)
        - normed * jnp.mean(scaled * normed, axis=0, keepdims=True)
    )


def gather_kernel(idx_ref, table_ref, out_ref):
    peers = out_ref.shape[0]
    depth = table_ref.shape[1]

    def body(q, carry):
        hot0 = one_hot(idx_ref[2 * q], depth)
        hot1 = one_hot(idx_ref[2 * q + 1], depth)
        picked = dot_nn(table_ref[...], jnp.concatenate([hot0, hot1], axis=1)).astype(BF16)
        out_ref[2 * q] = picked[:, :TILE]
        out_ref[2 * q + 1] = picked[:, TILE:]
        return carry

    lax.fori_loop(0, peers // 2, body, 0)


def fill_table(table, local_ref, mirror_ref):
    local_tiles = local_ref.shape[1] // TILE
    for t in range(local_tiles):
        table[t] = local_ref[:, t * TILE : (t + 1) * TILE]

    def body(p, carry):
        table[local_tiles + p] = mirror_ref[p, :TILE, :]
        return carry

    lax.fori_loop(0, mirror_ref.shape[0], body, 0)


def edge_fwd_kernel(
    tile_ref,
    count_ref,
    offset_ref,
    edge_ref,
    node_ref,
    mirror_ref,
    w1_ref,
    b1_ref,
    w2_ref,
    gain_ref,
    shift_ref,
    pair_ref,
    hidden_ref,
    slope_ref,
    normed_ref,
    inv_ref,
    local_ref,
    out_ref,
    table,
    total,
):
    step = pl.program_id(0)
    latent = edge_ref.shape[0]
    local_tiles = node_ref.shape[1] // TILE

    @pl.when(step == 0)
    def _():
        fill_table(table, node_ref, mirror_ref)
        total[...] = jnp.zeros_like(total)

    receiver_hot = []
    for j in range(GROUP):
        b = step * GROUP + j
        cols = slice(j * TILE, (j + 1) * TILE)
        hot_s = one_hot(offset_ref[j, 0:1, :], TILE)
        hot_r = one_hot(offset_ref[j, 1:2, :], TILE)
        receiver_hot.append(hot_r)
        pair_ref[:latent, cols] = dot_nn(table[tile_ref[b, 0]], hot_s).astype(BF16)
        pair_ref[latent:, cols] = dot_nn(table[tile_ref[b, 1]], hot_r).astype(BF16)
    pre = (
        dot_nn(w1_ref[:, :latent], edge_ref[...])
        + dot_nn(w1_ref[:, latent:], pair_ref[...])
        + b1_ref[...]
    )
    gate = sigmoid(pre)
    hidden = (pre * gate).astype(BF16)
    hidden_ref[...] = hidden
    slope_ref[...] = gate * (1.0 + pre * (1.0 - gate))
    normed, inverse = layer_norm(dot_nn(w2_ref[...], hidden))
    normed_ref[...] = normed
    inv_ref[...] = inverse
    message = gain_ref[...] * normed + shift_ref[...]
    lane = lax.broadcasted_iota(jnp.int32, (latent, TILE), 1)
    for j in range(GROUP):
        b = step * GROUP + j
        cols = slice(j * TILE, (j + 1) * TILE)
        kept = jnp.where(lane < count_ref[b], message[:, cols], 0.0).astype(BF16)
        tile = tile_ref[b, 1]
        total[tile] += dot_nt(kept, receiver_hot[j])

    @pl.when(step == pl.num_programs(0) - 1)
    def _():
        for t in range(local_tiles):
            local_ref[:, t * TILE : (t + 1) * TILE] = total[t]

        def body(p, carry):
            out_ref[p] = total[local_tiles + p].astype(BF16)
            return carry

        lax.fori_loop(0, out_ref.shape[0], body, 0)


def scatter_mirrors(total_ref, idx_ref, mirror_ref):
    depth = total_ref.shape[1]

    def body(q, carry):
        hot = jnp.concatenate(
            [one_hot(idx_ref[2 * q], depth), one_hot(idx_ref[2 * q + 1], depth)], axis=1
        )
        values = jnp.concatenate(
            [mirror_ref[2 * q, :TILE, :], mirror_ref[2 * q + 1, :TILE, :]], axis=1
        )
        total_ref[...] += dot_nt(values, hot)
        return carry

    lax.fori_loop(0, mirror_ref.shape[0] // 2, body, 0)


def row_sum(values):
    folded = values[:, :TILE]
    for start in range(TILE, values.shape[1], TILE):
        folded = folded + values[:, start : start + TILE]
    return jnp.sum(folded.T, axis=0, keepdims=True)


def node_kernel(
    idx_ref,
    local_ref,
    mirror_ref,
    node_ref,
    cot_ref,
    w1_ref,
    b1_ref,
    w2_ref,
    gain_ref,
    shift_ref,
    node_out_ref,
    base_ref,
    grad_agg_ref,
    out_ref,
    total,
    rows,
):
    latent = node_ref.shape[0]
    peers = out_ref.shape[0]
    depth = node_ref.shape[1]
    total[...] = local_ref[...]
    scatter_mirrors(total, idx_ref, mirror_ref)
    agg_low = total[...].astype(BF16)
    node_low = node_ref[...]
    pre = dot_nn(w1_ref[:, :latent], node_low) + dot_nn(w1_ref[:, latent:], agg_low) + b1_ref[...]
    gate = sigmoid(pre)
    hidden = (pre * gate).astype(BF16)
    normed, inverse = layer_norm(dot_nn(w2_ref[...], hidden))
    gain = gain_ref[...]
    node_out_ref[...] = (node_low.astype(F32) + gain * normed + shift_ref[...]).astype(BF16)
    upstream = cot_ref[...].astype(F32)
    grad_post = norm_back(upstream, normed, inverse, gain).astype(BF16)
    grad_full = dot_tn(w2_ref[...], grad_post) * (gate * (1.0 + pre * (1.0 - gate)))
    grad_pre = grad_full.astype(BF16)
    base_ref[...] = upstream + dot_tn(w1_ref[:, :latent], grad_pre)
    grad_agg_ref[...] = dot_tn(w1_ref[:, latent:], grad_pre).astype(BF16)
    rows[...] = jnp.zeros_like(rows)
    rows[0:latent, :] = dot_nt(grad_pre, node_low)
    rows[latent : 2 * latent, :] = dot_nt(grad_pre, agg_low)
    rows[2 * latent : 3 * latent, :] = dot_nt(grad_post, hidden)
    at = 3 * latent
    rows[at : at + 1, :] = row_sum(grad_full)
    rows[at + 1 : at + 2, :] = row_sum(upstream * normed)
    rows[at + 2 : at + 3, :] = row_sum(upstream)

    def body(q, carry):
        hot = jnp.concatenate(
            [one_hot(idx_ref[2 * q], depth), one_hot(idx_ref[2 * q + 1], depth)], axis=1
        )
        picked = dot_nn(grad_agg_ref[...], hot).astype(BF16)
        for k in range(2):
            p = 2 * q + k
            out_ref[p, :TILE, :] = picked[:, k * TILE : (k + 1) * TILE]
            start = pl.multiple_of(p * NODE_ROWS, NODE_ROWS)
            out_ref[p, TILE:, :] = rows[pl.ds(start, NODE_ROWS), :].astype(BF16)
        return carry

    lax.fori_loop(0, peers // 2, body, 0)


def edge_bwd_kernel(
    tile_ref,
    count_ref,
    offset_ref,
    edge_ref,
    pair_ref,
    hidden_ref,
    slope_ref,
    normed_ref,
    inv_ref,
    agg_ref,
    mirror_ref,
    base_ref,
    w1_ref,
    w2_ref,
    gain_ref,
    edge_grad_ref,
    local_ref,
    out_ref,
    table,
    total,
    grad_w1,
    grad_w2,
    sum_gain,
    sum_shift,
    sum_bias,
    rows,
):
    step = pl.program_id(0)
    latent = edge_ref.shape[0]
    local_tiles = agg_ref.shape[1] // TILE

    @pl.when(step == 0)
    def _():
        fill_table(table, agg_ref, mirror_ref)
        total[...] = jnp.zeros_like(total)
        grad_w1[...] = jnp.zeros_like(grad_w1)
        grad_w2[...] = jnp.zeros_like(grad_w2)
        sum_gain[...] = jnp.zeros_like(sum_gain)
        sum_shift[...] = jnp.zeros_like(sum_shift)
        sum_bias[...] = jnp.zeros_like(sum_bias)

    lane = lax.broadcasted_iota(jnp.int32, (latent, TILE), 1)
    hots = []
    picked = []
    for j in range(GROUP):
        b = step * GROUP + j
        hot_s = one_hot(offset_ref[j, 0:1, :], TILE)
        hot_r = one_hot(offset_ref[j, 1:2, :], TILE)
        hots.append((hot_s, hot_r))
        found = dot_nn(table[tile_ref[b, 1]], hot_r)
        picked.append(jnp.where(lane < count_ref[b], found, 0.0))
    upstream = jnp.concatenate(picked, axis=1)
    normed = normed_ref[...]
    weighted = upstream * normed
    grad_post = norm_back(upstream, normed, inv_ref[...], gain_ref[...]).astype(BF16)
    hidden = hidden_ref[...]
    grad_w2[...] += dot_nt(grad_post, hidden)
    grad_full = dot_tn(w2_ref[...], grad_post) * slope_ref[...]
    grad_pre = grad_full.astype(BF16)
    edge_grad_ref[...] = dot_tn(w1_ref[:, :latent], grad_pre).astype(BF16)
    grad_w1[:, :latent] += dot_nt(grad_pre, edge_ref[...])
    grad_w1[:, latent:] += dot_nt(grad_pre, pair_ref[...])
    for j in range(GROUP):
        b = step * GROUP + j
        cols = slice(j * TILE, (j + 1) * TILE)
        sum_gain[...] += weighted[:, cols]
        sum_shift[...] += upstream[:, cols]
        sum_bias[...] += grad_full[:, cols]
        hot_s, hot_r = hots[j]
        total[tile_ref[b, 0], :latent, :] += dot_nt(grad_pre[:, cols], hot_s)
        total[tile_ref[b, 1], latent:, :] += dot_nt(grad_pre[:, cols], hot_r)

    @pl.when(step == pl.num_programs(0) - 1)
    def _():
        for t in range(local_tiles):
            cols = slice(t * TILE, (t + 1) * TILE)
            back = dot_tn(w1_ref[:, latent : 2 * latent], total[t, :latent, :].astype(BF16))
            back += dot_tn(w1_ref[:, 2 * latent :], total[t, latent:, :].astype(BF16))
            local_ref[:, cols] = base_ref[:, cols] + back
        for c in range(3):
            rows[c * latent : (c + 1) * latent, :] = grad_w1[:, c * latent : (c + 1) * latent]
        rows[3 * latent : 4 * latent, :] = grad_w2[...]

        def body(p, carry):
            t = local_tiles + p
            back = dot_tn(w1_ref[:, latent : 2 * latent], total[t, :latent, :].astype(BF16))
            back += dot_tn(w1_ref[:, 2 * latent :], total[t, latent:, :].astype(BF16))
            out_ref[p, :TILE, :] = back.astype(BF16)
            start = pl.multiple_of(p * 16, 16)
            out_ref[p, TILE : TILE + 16, :] = rows[pl.ds(start, 16), :].astype(BF16)
            out_ref[p, TILE + 16 :, :] = jnp.zeros((EDGE_ROWS - 16, TILE), BF16)
            return carry

        lax.fori_loop(0, out_ref.shape[0], body, 0)
        tail = jnp.concatenate(
            [
                row_sum(sum_bias[...]),
                row_sum(sum_gain[...]),
                row_sum(sum_shift[...]),
                jnp.zeros((EDGE_ROWS - 19, TILE), F32),
            ],
            axis=0,
        )
        out_ref[0, TILE + 16 :, :] = tail.astype(BF16)


def final_kernel(idx_ref, local_ref, mirror_ref, out_ref):
    out_ref[...] = local_ref[...]
    scatter_mirrors(out_ref, idx_ref, mirror_ref)


def params_kernel(edge_scale, node_scale, all_ref, out_ref, edge_rows, node_rows):
    peers = all_ref.shape[0]
    for p in range(peers):
        edge_rows[p * 16 : (p + 1) * 16, :] = all_ref[p, :16, :].astype(F32) * edge_scale
        node_rows[p * NODE_ROWS : (p + 1) * NODE_ROWS, :] = (
            all_ref[p, EDGE_ROWS:, :].astype(F32) * node_scale
        )
    tail = all_ref[0, 16:EDGE_ROWS, :].astype(F32) * edge_scale
    n = TILE
    for c in range(3):
        out_ref[pl.ds(c, n, stride=3), :] = edge_rows[c * n : (c + 1) * n, :]
    out_ref[3 * n : 3 * n + 1, :] = tail[0:1]
    out_ref[3 * n + 1 : 4 * n + 1, :] = edge_rows[3 * n : 4 * n, :]
    out_ref[4 * n + 1 : 4 * n + 3, :] = tail[1:3]
    at = 4 * n + 3
    for c in range(2):
        out_ref[pl.ds(at + c, n, stride=2), :] = node_rows[c * n : (c + 1) * n, :]
    at += 2 * n
    out_ref[at : at + 1, :] = node_rows[3 * n : 3 * n + 1, :]
    out_ref[at + 1 : at + 1 + n, :] = node_rows[2 * n : 3 * n, :]
    out_ref[at + 1 + n : at + 3 + n, :] = node_rows[3 * n + 1 : 3 * n + 3, :]


VMEM = pl.BlockSpec(memory_space=pltpu.VMEM)
SMEM = pl.BlockSpec(memory_space=pltpu.SMEM)
PARAMS = pltpu.CompilerParams(vmem_limit_bytes=48 * 1024 * 1024)


def whole(kernel, out_shape, n_in, scratch, name):
    return pl.pallas_call(
        kernel,
        out_shape=out_shape,
        in_specs=[VMEM] * n_in,
        out_specs=jax.tree.map(lambda _: VMEM, out_shape),
        scratch_shapes=scratch,
        compiler_params=PARAMS,
        interpret=INTERPRET,
        name=name,
    )


def per_device(
    node_feat,
    edge_feat,
    route,
    block_tile,
    block_offset,
    block_count,
    w_edge1,
    bias_edge1,
    w_edge2,
    gain_edge,
    shift_edge,
    w_node1,
    bias_node1,
    w_node2,
    gain_node,
    shift_node,
    node_cot,
):
    latent, masters = node_feat.shape
    slots = edge_feat.shape[1]
    blocks = block_tile.shape[0]
    peers = lax.axis_size("cut")
    total_nodes = masters * peers
    total_edges = slots * peers
    tiles = masters // TILE + peers
    shape = jax.ShapeDtypeStruct

    def swap(values):
        return lax.all_to_all(values, "cut", split_axis=0, concat_axis=0, tiled=True)

    def column(vector):
        return vector[:, None]

    idx = swap(route[0][:, None, :])
    outgoing = whole(gather_kernel, shape((peers, latent, TILE), BF16), 2, [], "gather")(
        idx, node_feat
    )
    mirrors = swap(outgoing)

    steps = blocks // GROUP
    width = GROUP * TILE

    def full(dims):
        return pl.BlockSpec(dims, lambda i: (0,) * len(dims))

    def wide(height):
        return pl.BlockSpec((height, width), lambda i: (0, i))

    offsets = pl.BlockSpec((GROUP, 2, TILE), lambda i: (i, 0, 0))
    pair, hidden, slope, normed, inv, local_sum, returned = pl.pallas_call(
        edge_fwd_kernel,
        grid=(steps,),
        out_shape=(
            shape((2 * latent, slots), BF16),
            shape((latent, slots), BF16),
            shape((latent, slots), F32),
            shape((latent, slots), F32),
            shape((1, slots), F32),
            shape((latent, masters), F32),
            shape((peers, latent, TILE), BF16),
        ),
        in_specs=[
            SMEM,
            SMEM,
            offsets,
            wide(latent),
            full((latent, masters)),
            full((peers, latent, TILE)),
            full((latent, 3 * latent)),
            full((latent, 1)),
            full((latent, latent)),
            full((latent, 1)),
            full((latent, 1)),
        ],
        out_specs=(
            wide(2 * latent),
            wide(latent),
            wide(latent),
            wide(latent),
            wide(1),
            full((latent, masters)),
            full((peers, latent, TILE)),
        ),
        scratch_shapes=[
            pltpu.VMEM((tiles, latent, TILE), BF16),
            pltpu.VMEM((tiles, latent, TILE), F32),
        ],
        compiler_params=PARAMS,
        interpret=INTERPRET,
        name="edge_fwd",
    )(
        block_tile,
        block_count,
        block_offset,
        edge_feat,
        node_feat,
        mirrors,
        w_edge1,
        column(bias_edge1),
        w_edge2,
        column(gain_edge),
        column(shift_edge),
    )
    returned = swap(returned)

    node_out, base, grad_agg, outgoing = whole(
        node_kernel,
        (
            shape((latent, masters), BF16),
            shape((latent, masters), F32),
            shape((latent, masters), BF16),
            shape((peers, latent + NODE_ROWS, TILE), BF16),
        ),
        10,
        [pltpu.VMEM((latent, masters), F32), pltpu.VMEM((peers * NODE_ROWS, TILE), F32)],
        "node",
    )(
        idx,
        local_sum,
        returned,
        node_feat,
        node_cot,
        w_node1,
        column(bias_node1),
        w_node2,
        column(gain_node),
        column(shift_node),
    )
    mirrors = swap(outgoing)
    node_shard = jnp.sum(mirrors[:, latent:, :].astype(F32), axis=0).astype(BF16)

    edge_grad, local_grad, returned = pl.pallas_call(
        edge_bwd_kernel,
        grid=(steps,),
        out_shape=(
            shape((latent, slots), BF16),
            shape((latent, masters), F32),
            shape((peers, latent + EDGE_ROWS, TILE), BF16),
        ),
        in_specs=[
            SMEM,
            SMEM,
            offsets,
            wide(latent),
            wide(2 * latent),
            wide(latent),
            wide(latent),
            wide(latent),
            wide(1),
            full((latent, masters)),
            full((peers, latent + NODE_ROWS, TILE)),
            full((latent, masters)),
            full((latent, 3 * latent)),
            full((latent, latent)),
            full((latent, 1)),
        ],
        out_specs=(
            wide(latent),
            full((latent, masters)),
            full((peers, latent + EDGE_ROWS, TILE)),
        ),
        scratch_shapes=[
            pltpu.VMEM((tiles, latent, TILE), BF16),
            pltpu.VMEM((tiles, 2 * latent, TILE), F32),
            pltpu.VMEM((latent, 3 * latent), F32),
            pltpu.VMEM((latent, latent), F32),
            pltpu.VMEM((latent, TILE), F32),
            pltpu.VMEM((latent, TILE), F32),
            pltpu.VMEM((latent, TILE), F32),
            pltpu.VMEM((4 * latent, TILE), F32),
        ],
        compiler_params=PARAMS,
        interpret=INTERPRET,
        name="edge_bwd",
    )(
        block_tile,
        block_count,
        block_offset,
        edge_feat,
        pair,
        hidden,
        slope,
        normed,
        inv,
        grad_agg,
        mirrors,
        base,
        w_edge1,
        w_edge2,
        column(gain_edge),
    )
    returned = swap(returned)
    edge_shard = jnp.sum(returned[:, latent:, :].astype(F32), axis=0).astype(BF16)
    shard = jnp.concatenate([edge_shard, node_shard], axis=0)
    gathered = swap(jnp.broadcast_to(shard[None], (peers,) + shard.shape))
    node_grad = whole(final_kernel, shape((latent, masters), F32), 3, [], "final")(
        idx, local_grad, returned
    )
    param_rows = whole(
        functools.partial(
            params_kernel, 1.0 / math.sqrt(total_edges), 1.0 / math.sqrt(total_nodes)
        ),
        shape((902, TILE), F32),
        1,
        [pltpu.VMEM((peers * 16, TILE), F32), pltpu.VMEM((peers * NODE_ROWS, TILE), F32)],
        "params",
    )(gathered)
    return (node_out, node_grad, edge_grad, param_rows.reshape(-1))


def solution(mesh):
    nodes = P(None, ("dp", "cut"))
    rows = P(("dp", "cut"))
    in_specs = (nodes, nodes, rows, rows, rows, rows) + (P(),) * 10 + (nodes,)
    out_specs = (nodes, nodes, nodes, P("dp"))
    return jax.shard_map(
        per_device, mesh=mesh, in_specs=in_specs, out_specs=out_specs, check_vma=False
    )
```

```python
import functools
import math

import jax
import jax.numpy as jnp
from jax import lax
from jax.experimental import pallas as pl
from jax.experimental.pallas import tpu as pltpu
from jax.sharding import PartitionSpec as P

F32 = jnp.float32
BF16 = jnp.bfloat16
TILE = 128
GROUP = 8
WIDE = 4
NODE_ROWS = 16
EDGE_ROWS = 24
INTERPRET = False


def dot_nn(left, right):
    return lax.dot_general(left, right, (((1,), (0,)), ((), ())), preferred_element_type=F32)


def dot_nt(left, right):
    return lax.dot_general(left, right, (((1,), (1,)), ((), ())), preferred_element_type=F32)


def dot_tn(left, right):
    return lax.dot_general(left, right, (((0,), (0,)), ((), ())), preferred_element_type=F32)


def one_hot(index_row, depth):
    rows = lax.broadcasted_iota(jnp.int32, (depth, index_row.shape[1]), 0)
    return jnp.where(rows == index_row, 1.0, 0.0).astype(BF16)


def sigmoid(values):
    return 1.0 / (1.0 + jnp.exp(-values))


def one_hot_rows(index_columns, depth):
    lanes = lax.broadcasted_iota(jnp.int32, (index_columns.shape[0], depth), 1)
    return jnp.where(lanes == index_columns, 1.0, 0.0).astype(BF16)


def column(row_ref):
    return jnp.broadcast_to(row_ref[...], (8, row_ref.shape[1])).T[:, :1]


def layer_norm(values):
    centred = values - jnp.mean(values, axis=0, keepdims=True)
    inverse = lax.rsqrt(jnp.mean(centred * centred, axis=0, keepdims=True) + 1e-05)
    return centred * inverse, inverse


def norm_back(upstream, normed, inverse, gain):
    scaled = upstream * gain
    return inverse * (
        scaled
        - jnp.mean(scaled, axis=0, keepdims=True)
        - normed * jnp.mean(scaled * normed, axis=0, keepdims=True)
    )


def gather_peers(idx_ref, table, store):
    depth = table.shape[1]
    for q in range(0, idx_ref.shape[0], WIDE):
        index_row = jnp.concatenate([idx_ref[q + k] for k in range(WIDE)], axis=1)
        picked = dot_nn(table, one_hot(index_row, depth)).astype(BF16)
        for k in range(WIDE):
            store(q + k, picked[:, k * TILE : (k + 1) * TILE])


def gather_kernel(idx_ref, table_ref, out_ref):
    def store(p, values):
        out_ref[p] = values

    gather_peers(idx_ref, table_ref[...], store)


def fill_table(table, local_ref, mirror_ref):
    local_tiles = local_ref.shape[1] // TILE
    for t in range(local_tiles):
        table[t] = local_ref[:, t * TILE : (t + 1) * TILE]

    def body(p, carry):
        table[local_tiles + p] = mirror_ref[p, :TILE, :]
        return carry

    lax.fori_loop(0, mirror_ref.shape[0], body, 0)


def edge_fwd_kernel(
    tile_ref,
    count_ref,
    offset_ref,
    edge_ref,
    node_ref,
    mirror_ref,
    w1_ref,
    b1_ref,
    w2_ref,
    gain_ref,
    shift_ref,
    pair_ref,
    hidden_ref,
    slope_ref,
    normed_ref,
    inv_ref,
    local_ref,
    out_ref,
    table,
    total,
):
    step = pl.program_id(0)
    latent = edge_ref.shape[0]
    local_tiles = node_ref.shape[1] // TILE

    @pl.when(step == 0)
    def _():
        fill_table(table, node_ref, mirror_ref)
        total[...] = jnp.zeros_like(total)

    for j in range(GROUP):
        b = step * GROUP + j
        both = jnp.concatenate([offset_ref[j, 0:1, :], offset_ref[j, 1:2, :] + TILE], axis=1)
        tiles = jnp.concatenate([table[tile_ref[0, b]], table[tile_ref[1, b]]], axis=1)
        found = dot_nn(tiles, one_hot(both, 2 * TILE)).astype(BF16)
        cols = slice(j * TILE, (j + 1) * TILE)
        pair_ref[:latent, cols] = found[:, :TILE]
        pair_ref[latent:, cols] = found[:, TILE:]
    pre = (
        dot_nn(w1_ref[:, :latent], edge_ref[...])
        + dot_nn(w1_ref[:, latent:], pair_ref[...])
        + column(b1_ref)
    )
    gate = sigmoid(pre)
    hidden = (pre * gate).astype(BF16)
    hidden_ref[...] = hidden
    slope_ref[...] = gate * (1.0 + pre * (1.0 - gate))
    normed, inverse = layer_norm(dot_nn(w2_ref[...], hidden))
    normed_ref[...] = normed
    inv_ref[...] = inverse
    message = column(gain_ref) * normed + column(shift_ref)
    turned = offset_ref[:, 1, :].T
    lane = lax.broadcasted_iota(jnp.int32, (latent, TILE), 1)
    for j in range(GROUP):
        b = step * GROUP + j
        cols = slice(j * TILE, (j + 1) * TILE)
        kept = jnp.where(lane < count_ref[b], message[:, cols], 0.0).astype(BF16)
        tile = tile_ref[1, b]
        total[tile] += dot_nn(kept, one_hot_rows(turned[:, j : j + 1], TILE))

    @pl.when(step == pl.num_programs(0) - 1)
    def _():
        for t in range(local_tiles):
            local_ref[:, t * TILE : (t + 1) * TILE] = total[t]

        def body(p, carry):
            out_ref[p] = total[local_tiles + p].astype(BF16)
            return carry

        lax.fori_loop(0, out_ref.shape[0], body, 0)


def scatter_mirrors(total, idx_ref, mirror_ref):
    depth = total.shape[1]
    peers = idx_ref.shape[0]
    turned = jnp.concatenate([idx_ref[p] for p in range(peers)], axis=0).T
    for q in range(0, peers, WIDE):
        hot = jnp.concatenate(
            [one_hot_rows(turned[:, p : p + 1], depth) for p in range(q, q + WIDE)], axis=0
        )
        values = jnp.concatenate([mirror_ref[p, :TILE, :] for p in range(q, q + WIDE)], axis=1)
        total += dot_nn(values, hot)
    return total


def row_sum(values):
    folded = values[:, :TILE]
    for start in range(TILE, values.shape[1], TILE):
        folded = folded + values[:, start : start + TILE]
    return jnp.sum(folded.T, axis=0, keepdims=True)


def node_kernel(
    idx_ref,
    local_ref,
    mirror_ref,
    node_ref,
    cot_ref,
    w1_ref,
    b1_ref,
    w2_ref,
    gain_ref,
    shift_ref,
    node_out_ref,
    base_ref,
    grad_agg_ref,
    out_ref,
    rows,
):
    latent = node_ref.shape[0]
    agg_low = scatter_mirrors(local_ref[...], idx_ref, mirror_ref).astype(BF16)
    node_low = node_ref[...]
    pre = dot_nn(w1_ref[:, :latent], node_low) + dot_nn(w1_ref[:, latent:], agg_low) + column(b1_ref)
    gate = sigmoid(pre)
    hidden = (pre * gate).astype(BF16)
    normed, inverse = layer_norm(dot_nn(w2_ref[...], hidden))
    gain = column(gain_ref)
    node_out_ref[...] = (node_low.astype(F32) + gain * normed + column(shift_ref)).astype(BF16)
    upstream = cot_ref[...].astype(F32)
    grad_post = norm_back(upstream, normed, inverse, gain).astype(BF16)
    grad_full = dot_tn(w2_ref[...], grad_post) * (gate * (1.0 + pre * (1.0 - gate)))
    grad_pre = grad_full.astype(BF16)
    base_ref[...] = upstream + dot_tn(w1_ref[:, :latent], grad_pre)
    grad_agg_ref[...] = dot_tn(w1_ref[:, latent:], grad_pre).astype(BF16)
    rows[...] = jnp.zeros_like(rows)
    rows[0:latent, :] = dot_nt(grad_pre, node_low)
    rows[latent : 2 * latent, :] = dot_nt(grad_pre, agg_low)
    rows[2 * latent : 3 * latent, :] = dot_nt(grad_post, hidden)
    at = 3 * latent
    rows[at : at + 1, :] = row_sum(grad_full)
    rows[at + 1 : at + 2, :] = row_sum(upstream * normed)
    rows[at + 2 : at + 3, :] = row_sum(upstream)

    def store(p, values):
        out_ref[p, :TILE, :] = values
        out_ref[p, TILE:, :] = rows[p * NODE_ROWS : (p + 1) * NODE_ROWS, :].astype(BF16)

    gather_peers(idx_ref, grad_agg_ref[...], store)


def edge_bwd_kernel(
    tile_ref,
    count_ref,
    offset_ref,
    edge_ref,
    pair_ref,
    hidden_ref,
    slope_ref,
    normed_ref,
    inv_ref,
    agg_ref,
    mirror_ref,
    base_ref,
    w1_ref,
    w2_ref,
    gain_ref,
    edge_grad_ref,
    local_ref,
    out_ref,
    table,
    total,
    grad_w1,
    grad_w2,
    sum_gain,
    sum_shift,
    sum_bias,
    rows,
    w1_turned,
    w1_pair,
    w2_turned,
):
    step = pl.program_id(0)
    latent = edge_ref.shape[0]
    local_tiles = agg_ref.shape[1] // TILE

    @pl.when(step == 0)
    def _():
        fill_table(table, agg_ref, mirror_ref)
        total[...] = jnp.zeros_like(total)
        grad_w1[...] = jnp.zeros_like(grad_w1)
        grad_w2[...] = jnp.zeros_like(grad_w2)
        sum_gain[...] = jnp.zeros_like(sum_gain)
        sum_shift[...] = jnp.zeros_like(sum_shift)
        sum_bias[...] = jnp.zeros_like(sum_bias)
        w2_turned[...] = w2_ref[...].T
        w1_turned[...] = w1_ref[:, :latent].T
        w1_pair[:, :latent] = w1_ref[:, latent : 2 * latent].T
        w1_pair[:, latent:] = w1_ref[:, 2 * latent :].T

    lane = lax.broadcasted_iota(jnp.int32, (latent, TILE), 1)
    picked = []
    for j in range(GROUP):
        b = step * GROUP + j
        found = dot_nn(table[tile_ref[1, b]], one_hot(offset_ref[j, 1:2, :], TILE))
        picked.append(jnp.where(lane < count_ref[b], found, 0.0))
    upstream = jnp.concatenate(picked, axis=1)
    normed = normed_ref[...]
    weighted = upstream * normed
    grad_post = norm_back(upstream, normed, inv_ref[...], column(gain_ref)).astype(BF16)
    hidden = hidden_ref[...]
    grad_full = dot_nn(w2_turned[...], grad_post) * slope_ref[...]
    grad_pre = grad_full.astype(BF16)
    edge_grad_ref[...] = dot_nn(w1_turned[...], grad_pre).astype(BF16)
    senders = offset_ref[:, 0, :].T
    receivers = offset_ref[:, 1, :].T
    gain_part, shift_part, bias_part = sum_gain[...], sum_shift[...], sum_bias[...]
    for j in range(GROUP):
        b = step * GROUP + j
        cols = slice(j * TILE, (j + 1) * TILE)
        gain_part += weighted[:, cols]
        shift_part += upstream[:, cols]
        bias_part += grad_full[:, cols]
        hot = jnp.concatenate(
            [
                one_hot_rows(senders[:, j : j + 1], TILE),
                one_hot_rows(receivers[:, j : j + 1], TILE),
            ],
            axis=1,
        )
        spread = dot_nn(grad_pre[:, cols], hot)
        total[tile_ref[0, b], :latent, :] += spread[:, :TILE]
        total[tile_ref[1, b], latent:, :] += spread[:, TILE:]
    sum_gain[...], sum_shift[...], sum_bias[...] = gain_part, shift_part, bias_part
    grad_w2[...] += dot_nt(grad_post, hidden)
    grad_w1[:, :latent] += dot_nt(grad_pre, edge_ref[...])
    grad_w1[:, latent:] += dot_nt(grad_pre, pair_ref[...])

    @pl.when(step == pl.num_programs(0) - 1)
    def _():
        for c in range(3):
            rows[c * latent : (c + 1) * latent, :] = grad_w1[:, c * latent : (c + 1) * latent]
        rows[3 * latent : 4 * latent, :] = grad_w2[...]
        for t in range(0, table.shape[0], WIDE):
            group = range(t, t + WIDE)
            low = jnp.concatenate([total[k].astype(BF16) for k in group], axis=1)
            back = dot_nn(w1_pair[...], low)
            for k in group:
                part = back[:, (k - t) * TILE : (k - t + 1) * TILE]
                if k < local_tiles:
                    cols = slice(k * TILE, (k + 1) * TILE)
                    local_ref[:, cols] = base_ref[:, cols] + part
                else:
                    p = k - local_tiles
                    out_ref[p, :TILE, :] = part.astype(BF16)
                    out_ref[p, TILE : TILE + 16, :] = rows[p * 16 : p * 16 + 16, :].astype(BF16)
                    out_ref[p, TILE + 16 :, :] = jnp.zeros((EDGE_ROWS - 16, TILE), BF16)
        tail = jnp.concatenate(
            [
                row_sum(sum_bias[...]),
                row_sum(sum_gain[...]),
                row_sum(sum_shift[...]),
                jnp.zeros((EDGE_ROWS - 19, TILE), F32),
            ],
            axis=0,
        )
        out_ref[0, TILE + 16 :, :] = tail.astype(BF16)


def final_kernel(idx_ref, local_ref, mirror_ref, out_ref):
    out_ref[...] = scatter_mirrors(local_ref[...], idx_ref, mirror_ref)


def params_kernel(edge_scale, node_scale, all_ref, out_ref, edge_rows, node_rows):
    peers = all_ref.shape[0]
    for p in range(peers):
        edge_rows[p * 16 : (p + 1) * 16, :] = all_ref[p, :16, :].astype(F32) * edge_scale
        node_rows[p * NODE_ROWS : (p + 1) * NODE_ROWS, :] = (
            all_ref[p, EDGE_ROWS:, :].astype(F32) * node_scale
        )
    tail = all_ref[0, 16:EDGE_ROWS, :].astype(F32) * edge_scale
    n = TILE
    for c in range(3):
        out_ref[pl.ds(c, n, stride=3), :] = edge_rows[c * n : (c + 1) * n, :]
    out_ref[3 * n : 3 * n + 1, :] = tail[0:1]
    out_ref[3 * n + 1 : 4 * n + 1, :] = edge_rows[3 * n : 4 * n, :]
    out_ref[4 * n + 1 : 4 * n + 3, :] = tail[1:3]
    at = 4 * n + 3
    for c in range(2):
        out_ref[pl.ds(at + c, n, stride=2), :] = node_rows[c * n : (c + 1) * n, :]
    at += 2 * n
    out_ref[at : at + 1, :] = node_rows[3 * n : 3 * n + 1, :]
    out_ref[at + 1 : at + 1 + n, :] = node_rows[2 * n : 3 * n, :]
    out_ref[at + 1 + n : at + 3 + n, :] = node_rows[3 * n + 1 : 3 * n + 3, :]


VMEM = pl.BlockSpec(memory_space=pltpu.VMEM)
SMEM = pl.BlockSpec(memory_space=pltpu.SMEM)
PARAMS = pltpu.CompilerParams(vmem_limit_bytes=40 * 1024 * 1024)


def whole(kernel, out_shape, n_in, scratch, name):
    return pl.pallas_call(
        kernel,
        out_shape=out_shape,
        in_specs=[VMEM] * n_in,
        out_specs=jax.tree.map(lambda _: VMEM, out_shape),
        scratch_shapes=scratch,
        compiler_params=PARAMS,
        interpret=INTERPRET,
        name=name,
    )


def per_device(
    node_feat,
    edge_feat,
    route,
    block_tile,
    block_offset,
    block_count,
    w_edge1,
    bias_edge1,
    w_edge2,
    gain_edge,
    shift_edge,
    w_node1,
    bias_node1,
    w_node2,
    gain_node,
    shift_node,
    node_cot,
):
    latent, masters = node_feat.shape
    slots = edge_feat.shape[1]
    blocks = block_tile.shape[0]
    peers = lax.axis_size("cut")
    total_nodes = masters * peers
    total_edges = slots * peers
    tiles = masters // TILE + peers
    shape = jax.ShapeDtypeStruct

    def swap(values):
        return lax.all_to_all(values, "cut", split_axis=0, concat_axis=0, tiled=True)

    def near(values):
        return pltpu.with_memory_space_constraint(values, pltpu.VMEM)

    def hbm(values):
        return pltpu.with_memory_space_constraint(values, pltpu.HBM)

    def sent(dims, dtype):
        return pltpu.HBM(dims, dtype)

    def row(vector):
        return hbm(vector[None, :])

    idx = swap(route[0][:, None, :])
    outgoing = whole(gather_kernel, sent((peers, latent, TILE), BF16), 2, [], "gather")(
        near(idx), hbm(node_feat)
    )
    mirrors = swap(outgoing)

    steps = blocks // GROUP
    width = GROUP * TILE

    def full(dims):
        return pl.BlockSpec(dims, lambda i: (0,) * len(dims))

    def wide(height):
        return pl.BlockSpec((height, width), lambda i: (0, i))

    offsets = pl.BlockSpec((GROUP, 2, TILE), lambda i: (i, 0, 0))
    pair, hidden, slope, normed, inv, local_sum, returned = pl.pallas_call(
        edge_fwd_kernel,
        grid=(steps,),
        out_shape=(
            sent((2 * latent, slots), BF16),
            sent((latent, slots), BF16),
            sent((latent, slots), F32),
            sent((latent, slots), F32),
            sent((1, slots), F32),
            sent((latent, masters), F32),
            sent((peers, latent, TILE), BF16),
        ),
        in_specs=[
            SMEM,
            SMEM,
            offsets,
            wide(latent),
            full((latent, masters)),
            full((peers, latent, TILE)),
            full((latent, 3 * latent)),
            full((1, latent)),
            full((latent, latent)),
            full((1, latent)),
            full((1, latent)),
        ],
        out_specs=(
            wide(2 * latent),
            wide(latent),
            wide(latent),
            wide(latent),
            wide(1),
            full((latent, masters)),
            full((peers, latent, TILE)),
        ),
        scratch_shapes=[
            pltpu.VMEM((tiles, latent, TILE), BF16),
            pltpu.VMEM((tiles, latent, TILE), F32),
        ],
        compiler_params=PARAMS,
        interpret=INTERPRET,
        name="edge_fwd",
    )(
        hbm(block_tile.T),
        hbm(block_count),
        hbm(block_offset),
        hbm(edge_feat),
        hbm(node_feat),
        near(mirrors),
        hbm(w_edge1),
        row(bias_edge1),
        hbm(w_edge2),
        row(gain_edge),
        row(shift_edge),
    )
    returned = swap(returned)

    node_out, base, grad_agg, outgoing = whole(
        node_kernel,
        (
            sent((latent, masters), BF16),
            sent((latent, masters), F32),
            sent((latent, masters), BF16),
            sent((peers, latent + NODE_ROWS, TILE), BF16),
        ),
        10,
        [pltpu.VMEM((peers * NODE_ROWS, TILE), F32)],
        "node",
    )(
        near(idx),
        hbm(local_sum),
        near(returned),
        hbm(node_feat),
        hbm(node_cot),
        hbm(w_node1),
        row(bias_node1),
        hbm(w_node2),
        row(gain_node),
        row(shift_node),
    )
    mirrors = swap(outgoing)
    node_shard = jnp.sum(mirrors[:, latent:, :].astype(F32), axis=0).astype(BF16)

    edge_grad, local_grad, returned = pl.pallas_call(
        edge_bwd_kernel,
        grid=(steps,),
        out_shape=(
            sent((latent, slots), BF16),
            sent((latent, masters), F32),
            sent((peers, latent + EDGE_ROWS, TILE), BF16),
        ),
        in_specs=[
            SMEM,
            SMEM,
            offsets,
            wide(latent),
            wide(2 * latent),
            wide(latent),
            wide(latent),
            wide(latent),
            wide(1),
            full((latent, masters)),
            full((peers, latent + NODE_ROWS, TILE)),
            full((latent, masters)),
            full((latent, 3 * latent)),
            full((latent, latent)),
            full((1, latent)),
        ],
        out_specs=(
            wide(latent),
            full((latent, masters)),
            full((peers, latent + EDGE_ROWS, TILE)),
        ),
        scratch_shapes=[
            pltpu.VMEM((tiles, latent, TILE), BF16),
            pltpu.VMEM((tiles, 2 * latent, TILE), F32),
            pltpu.VMEM((latent, 3 * latent), F32),
            pltpu.VMEM((latent, latent), F32),
            pltpu.VMEM((latent, TILE), F32),
            pltpu.VMEM((latent, TILE), F32),
            pltpu.VMEM((latent, TILE), F32),
            pltpu.VMEM((4 * latent, TILE), F32),
            pltpu.VMEM((latent, latent), BF16),
            pltpu.VMEM((latent, 2 * latent), BF16),
            pltpu.VMEM((latent, latent), BF16),
        ],
        compiler_params=PARAMS,
        interpret=INTERPRET,
        name="edge_bwd",
    )(
        hbm(block_tile.T),
        hbm(block_count),
        hbm(block_offset),
        hbm(edge_feat),
        hbm(pair),
        hbm(hidden),
        hbm(slope),
        hbm(normed),
        hbm(inv),
        hbm(grad_agg),
        near(mirrors),
        hbm(base),
        hbm(w_edge1),
        hbm(w_edge2),
        row(gain_edge),
    )
    returned = swap(returned)
    edge_shard = jnp.sum(returned[:, latent:, :].astype(F32), axis=0).astype(BF16)
    shard = jnp.concatenate([edge_shard, node_shard], axis=0)
    gathered = swap(jnp.broadcast_to(shard[None], (peers,) + shard.shape))
    node_grad = whole(final_kernel, sent((latent, masters), F32), 3, [], "final")(
        near(idx), hbm(local_grad), near(returned)
    )
    param_rows = whole(
        functools.partial(
            params_kernel, 1.0 / math.sqrt(total_edges), 1.0 / math.sqrt(total_nodes)
        ),
        sent((902, TILE), F32),
        1,
        [pltpu.VMEM((peers * 16, TILE), F32), pltpu.VMEM((peers * NODE_ROWS, TILE), F32)],
        "params",
    )(near(gathered))
    return (node_out, node_grad, edge_grad, param_rows.reshape(-1))


def solution(mesh):
    nodes = P(None, ("dp", "cut"))
    rows = P(("dp", "cut"))
    in_specs = (nodes, nodes, rows, rows, rows, rows) + (P(),) * 10 + (nodes,)
    out_specs = (nodes, nodes, nodes, P("dp"))
    return jax.shard_map(
        per_device, mesh=mesh, in_specs=in_specs, out_specs=out_specs, check_vma=False
    )
```

```python
import functools
import math

import jax
import jax.numpy as jnp
from jax import lax
from jax.experimental import pallas as pl
from jax.experimental.pallas import tpu as pltpu
from jax.sharding import PartitionSpec as P

F32 = jnp.float32
BF16 = jnp.bfloat16
TILE = 128
GROUP = 16
WIDE = 4
QUARTER = 232
INTERPRET = False


def dot_nn(left, right):
    return lax.dot_general(left, right, (((1,), (0,)), ((), ())), preferred_element_type=F32)


def dot_nt(left, right):
    return lax.dot_general(left, right, (((1,), (1,)), ((), ())), preferred_element_type=F32)


def dot_tn(left, right):
    return lax.dot_general(left, right, (((0,), (0,)), ((), ())), preferred_element_type=F32)


def one_hot(index_row, depth):
    rows = lax.broadcasted_iota(jnp.int32, (depth, index_row.shape[1]), 0)
    return jnp.where(rows == index_row, 1.0, 0.0).astype(BF16)


def sigmoid(values):
    return 1.0 / (1.0 + jnp.exp(-values))


def one_hot_rows(index_columns, depth):
    lanes = lax.broadcasted_iota(jnp.int32, (index_columns.shape[0], depth), 1)
    return jnp.where(lanes == index_columns, 1.0, 0.0).astype(BF16)


def column(row_ref):
    return jnp.broadcast_to(row_ref[...], (8, row_ref.shape[1])).T[:, :1]


def layer_norm(values):
    centred = values - jnp.mean(values, axis=0, keepdims=True)
    inverse = lax.rsqrt(jnp.mean(centred * centred, axis=0, keepdims=True) + 1e-05)
    return centred * inverse, inverse


def norm_back(upstream, normed, inverse, gain):
    scaled = upstream * gain
    return inverse * (
        scaled
        - jnp.mean(scaled, axis=0, keepdims=True)
        - normed * jnp.mean(scaled * normed, axis=0, keepdims=True)
    )


def gather_peers(idx_ref, table, store):
    depth = table.shape[1]
    for q in range(0, idx_ref.shape[0], WIDE):
        index_row = jnp.concatenate([idx_ref[q + k] for k in range(WIDE)], axis=1)
        picked = dot_nn(table, one_hot(index_row, depth)).astype(BF16)
        for k in range(WIDE):
            store(q + k, picked[:, k * TILE : (k + 1) * TILE])


def gather_kernel(idx_ref, table_ref, out_ref):
    def store(p, values):
        out_ref[p] = values

    gather_peers(idx_ref, table_ref[...], store)


def fill_table(table, local_ref, mirror_ref):
    local_tiles = local_ref.shape[1] // TILE
    for t in range(local_tiles):
        table[t] = local_ref[:, t * TILE : (t + 1) * TILE]

    def body(p, carry):
        table[local_tiles + p] = mirror_ref[p, :TILE, :]
        return carry

    lax.fori_loop(0, mirror_ref.shape[0], body, 0)


def edge_network(step, tile_ref, offset_ref, edge_ref, table, w1_ref, b1_ref, w2_ref):
    latent = edge_ref.shape[0]
    pairs = []
    for j in range(GROUP):
        b = step * GROUP + j
        both = jnp.concatenate([offset_ref[j, 0:1, :], offset_ref[j, 1:2, :] + TILE], axis=1)
        tiles = jnp.concatenate([table[tile_ref[0, b]], table[tile_ref[1, b]]], axis=1)
        found = dot_nn(tiles, one_hot(both, 2 * TILE)).astype(BF16)
        pairs.append(jnp.concatenate([found[:, :TILE], found[:, TILE:]], axis=0))
    pair = jnp.concatenate(pairs, axis=1)
    pre = (
        dot_nn(w1_ref[:, :latent], edge_ref[...])
        + dot_nn(w1_ref[:, latent:], pair)
        + column(b1_ref)
    )
    gate = sigmoid(pre)
    hidden = (pre * gate).astype(BF16)
    normed, inverse = layer_norm(dot_nn(w2_ref[...], hidden))
    return pair, pre, gate, hidden, normed, inverse


def edge_fwd_kernel(
    tile_ref,
    count_ref,
    offset_ref,
    edge_ref,
    node_ref,
    mirror_ref,
    w1_ref,
    b1_ref,
    w2_ref,
    gain_ref,
    shift_ref,
    local_ref,
    out_ref,
    table,
    total,
):
    step = pl.program_id(0)
    latent = edge_ref.shape[0]
    local_tiles = node_ref.shape[1] // TILE

    @pl.when(step == 0)
    def _():
        fill_table(table, node_ref, mirror_ref)
        total[...] = jnp.zeros_like(total)

    normed = edge_network(step, tile_ref, offset_ref, edge_ref, table, w1_ref, b1_ref, w2_ref)[4]
    message = column(gain_ref) * normed + column(shift_ref)
    turned = offset_ref[:, 1, :].T
    lane = lax.broadcasted_iota(jnp.int32, (latent, TILE), 1)
    spread = []
    for j in range(GROUP):
        values = message[:, j * TILE : (j + 1) * TILE]
        kept = jnp.where(lane < count_ref[step * GROUP + j], values, 0.0).astype(BF16)
        spread.append(dot_nn(kept, one_hot_rows(turned[:, j : j + 1], TILE)))
    for j in range(GROUP):
        total[tile_ref[1, step * GROUP + j]] += spread[j]

    @pl.when(step == pl.num_programs(0) - 1)
    def _():
        for t in range(local_tiles):
            local_ref[:, t * TILE : (t + 1) * TILE] = total[t]

        def body(p, carry):
            out_ref[p] = total[local_tiles + p].astype(BF16)
            return carry

        lax.fori_loop(0, out_ref.shape[0], body, 0)


def edge_keep_kernel(
    tile_ref,
    offset_ref,
    edge_ref,
    node_ref,
    mirror_ref,
    w1_ref,
    b1_ref,
    w2_ref,
    pair_ref,
    hidden_ref,
    slope_ref,
    normed_ref,
    inv_ref,
    table,
):
    step = pl.program_id(0)

    @pl.when(step == 0)
    def _():
        fill_table(table, node_ref, mirror_ref)

    pair, pre, gate, hidden, normed, inverse = edge_network(
        step, tile_ref, offset_ref, edge_ref, table, w1_ref, b1_ref, w2_ref
    )
    pair_ref[...] = pair
    hidden_ref[...] = hidden
    slope_ref[...] = gate * (1.0 + pre * (1.0 - gate))
    normed_ref[...] = normed
    inv_ref[...] = inverse


def scatter_mirrors(total, idx_ref, mirror_ref):
    depth = total.shape[1]
    peers = idx_ref.shape[0]
    turned = jnp.concatenate([idx_ref[p] for p in range(peers)], axis=0).T
    for q in range(0, peers, WIDE):
        hot = jnp.concatenate(
            [one_hot_rows(turned[:, p : p + 1], depth) for p in range(q, q + WIDE)], axis=0
        )
        values = jnp.concatenate([mirror_ref[p, :TILE, :] for p in range(q, q + WIDE)], axis=1)
        total += dot_nn(values, hot)
    return total


def row_sum(values):
    folded = values[:, :TILE]
    for start in range(TILE, values.shape[1], TILE):
        folded = folded + values[:, start : start + TILE]
    return jnp.sum(folded.T, axis=0, keepdims=True)


def node_network(node_low, agg_low, cot_ref, w1_ref, b1_ref, w2_ref, gain):
    latent = node_low.shape[0]
    pre = dot_nn(w1_ref[:, :latent], node_low) + dot_nn(w1_ref[:, latent:], agg_low) + column(b1_ref)
    gate = sigmoid(pre)
    hidden = (pre * gate).astype(BF16)
    normed, inverse = layer_norm(dot_nn(w2_ref[...], hidden))
    upstream = cot_ref[...].astype(F32)
    grad_post = norm_back(upstream, normed, inverse, gain).astype(BF16)
    grad_full = dot_tn(w2_ref[...], grad_post) * (gate * (1.0 + pre * (1.0 - gate)))
    return hidden, normed, upstream, grad_post, grad_full


def node_kernel(
    idx_ref,
    local_ref,
    mirror_ref,
    node_ref,
    cot_ref,
    w1_ref,
    b1_ref,
    w2_ref,
    gain_ref,
    agg_low_ref,
    grad_agg_ref,
    out_ref,
):
    latent = node_ref.shape[0]
    agg_low = scatter_mirrors(local_ref[...], idx_ref, mirror_ref).astype(BF16)
    agg_low_ref[...] = agg_low
    grad_full = node_network(
        node_ref[...], agg_low, cot_ref, w1_ref, b1_ref, w2_ref, column(gain_ref)
    )[4]
    grad_agg = dot_tn(w1_ref[:, latent:], grad_full.astype(BF16)).astype(BF16)
    grad_agg_ref[...] = grad_agg

    def store(p, values):
        out_ref[p] = values

    gather_peers(idx_ref, grad_agg, store)


def node_rest_kernel(
    agg_low_ref,
    node_ref,
    cot_ref,
    w1_ref,
    b1_ref,
    w2_ref,
    gain_ref,
    shift_ref,
    node_out_ref,
    base_ref,
    rows,
):
    latent = node_ref.shape[0]
    node_low, agg_low, gain = node_ref[...], agg_low_ref[...], column(gain_ref)
    hidden, normed, upstream, grad_post, grad_full = node_network(
        node_low, agg_low, cot_ref, w1_ref, b1_ref, w2_ref, gain
    )
    grad_pre = grad_full.astype(BF16)
    node_out_ref[...] = (node_low.astype(F32) + gain * normed + column(shift_ref)).astype(BF16)
    base_ref[...] = upstream + dot_tn(w1_ref[:, :latent], grad_pre)
    rows[0:latent, :] = dot_nt(grad_pre, node_low)
    rows[latent : 2 * latent, :] = dot_nt(grad_pre, agg_low)
    rows[2 * latent : 3 * latent, :] = dot_nt(grad_post, hidden)
    sums = [row_sum(grad_full), row_sum(upstream * normed), row_sum(upstream)]
    rows[3 * latent :, :] = jnp.concatenate(sums + [jnp.zeros((5, TILE), F32)], axis=0)


def edge_bwd_kernel(
    tile_ref,
    count_ref,
    offset_ref,
    slope_ref,
    normed_ref,
    inv_ref,
    agg_ref,
    mirror_ref,
    base_ref,
    w1_ref,
    w2_ref,
    gain_ref,
    post_ref,
    pre_ref,
    local_ref,
    out_ref,
    sums_ref,
    table,
    total,
    sums,
    w1_pair,
    w2_turned,
):
    step = pl.program_id(0)
    latent = slope_ref.shape[0]
    local_tiles = agg_ref.shape[1] // TILE

    @pl.when(step == 0)
    def _():
        fill_table(table, agg_ref, mirror_ref)
        total[...] = jnp.zeros_like(total)
        sums[...] = jnp.zeros_like(sums)
        w2_turned[...] = w2_ref[...].T
        w1_pair[:, :latent] = w1_ref[:, latent : 2 * latent].T
        w1_pair[:, latent:] = w1_ref[:, 2 * latent :].T

    lane = lax.broadcasted_iota(jnp.int32, (latent, TILE), 1)
    gain = column(gain_ref)
    senders = offset_ref[:, 0, :].T
    receivers = offset_ref[:, 1, :].T
    bias_part, gain_part, shift_part = sums[0], sums[1], sums[2]
    picked = []
    for j in range(GROUP):
        b = step * GROUP + j
        found = dot_nn(table[tile_ref[1, b]], one_hot(offset_ref[j, 1:2, :], TILE))
        picked.append(jnp.where(lane < count_ref[b], found, 0.0))
    upstream = jnp.concatenate(picked, axis=1)
    normed = normed_ref[...]
    weighted = upstream * normed
    grad_post = norm_back(upstream, normed, inv_ref[...], gain).astype(BF16)
    post_ref[...] = grad_post
    grad_full = dot_nn(w2_turned[...], grad_post) * slope_ref[...]
    grad_pre = grad_full.astype(BF16)
    pre_ref[...] = grad_pre
    spread = []
    for j in range(GROUP):
        cols = slice(j * TILE, (j + 1) * TILE)
        bias_part += grad_full[:, cols]
        gain_part += weighted[:, cols]
        shift_part += upstream[:, cols]
        hot = jnp.concatenate(
            [
                one_hot_rows(senders[:, j : j + 1], TILE),
                one_hot_rows(receivers[:, j : j + 1], TILE),
            ],
            axis=1,
        )
        spread.append(dot_nn(grad_pre[:, cols], hot))
    for j in range(GROUP):
        b = step * GROUP + j
        total[tile_ref[0, b], :latent, :] += spread[j][:, :TILE]
        total[tile_ref[1, b], latent:, :] += spread[j][:, TILE:]
    sums[0], sums[1], sums[2] = bias_part, gain_part, shift_part

    @pl.when(step == pl.num_programs(0) - 1)
    def _():
        sums_ref[...] = sums[...]
        for t in range(0, table.shape[0], WIDE):
            group = range(t, t + WIDE)
            low = jnp.concatenate([total[k].astype(BF16) for k in group], axis=1)
            back = dot_nn(w1_pair[...], low)
            for k in group:
                part = back[:, (k - t) * TILE : (k - t + 1) * TILE]
                if k < local_tiles:
                    cols = slice(k * TILE, (k + 1) * TILE)
                    local_ref[:, cols] = base_ref[:, cols] + part
                else:
                    out_ref[k - local_tiles] = part.astype(BF16)


def edge_weights_kernel(
    edge_ref,
    pair_ref,
    hidden_ref,
    post_ref,
    pre_ref,
    w1_ref,
    sums_ref,
    node_rows_ref,
    edge_grad_ref,
    rows_ref,
    grad_w1,
    grad_w2,
    w1_turned,
):
    step = pl.program_id(0)
    latent = edge_ref.shape[0]

    @pl.when(step == 0)
    def _():
        grad_w1[...] = jnp.zeros_like(grad_w1)
        grad_w2[...] = jnp.zeros_like(grad_w2)
        w1_turned[...] = w1_ref[:, :latent].T

    grad_pre = pre_ref[...]
    edge_grad_ref[...] = dot_nn(w1_turned[...], grad_pre).astype(BF16)
    grad_w2[...] += dot_nt(post_ref[...], hidden_ref[...])
    grad_w1[:latent] += dot_nt(edge_ref[...], grad_pre)
    grad_w1[latent:] += dot_nt(pair_ref[...], grad_pre)

    @pl.when(step == pl.num_programs(0) - 1)
    def _():
        n = latent
        for c in range(3):
            rows_ref[c * n : (c + 1) * n, :] = grad_w1[c * n : (c + 1) * n, :].T.astype(BF16)
        rows_ref[3 * n : 4 * n, :] = grad_w2[...].astype(BF16)
        rows_ref[4 * n : 7 * n, :] = node_rows_ref[: 3 * n, :].astype(BF16)
        tail = [row_sum(sums_ref[k]) for k in range(3)]
        tail += [node_rows_ref[3 * n : 3 * n + 3, :], jnp.zeros((26, TILE), F32)]
        rows_ref[7 * n :, :] = jnp.concatenate(tail, axis=0).astype(BF16)


def final_kernel(idx_ref, local_ref, mirror_ref, out_ref):
    out_ref[...] = scatter_mirrors(local_ref[...], idx_ref, mirror_ref)


def params_kernel(edge_scale, node_scale, place_ref, quarters_ref, out_ref, flat):
    for q in range(4):
        rows = quarters_ref[(place_ref[0] - q) & 3]
        flat[q * QUARTER : (q + 1) * QUARTER, :] = rows.astype(F32)
    n = TILE
    tail = flat[7 * n : 7 * n + 8, :]
    for c in range(3):
        out_ref[pl.ds(c, n, stride=3), :] = flat[c * n : (c + 1) * n, :] * edge_scale
    out_ref[3 * n : 3 * n + 1, :] = tail[0:1] * edge_scale
    out_ref[3 * n + 1 : 4 * n + 1, :] = flat[3 * n : 4 * n, :] * edge_scale
    out_ref[4 * n + 1 : 4 * n + 3, :] = tail[1:3] * edge_scale
    at = 4 * n + 3
    for c in range(2):
        rows = flat[(4 + c) * n : (5 + c) * n, :]
        out_ref[pl.ds(at + c, n, stride=2), :] = rows * node_scale
    at += 2 * n
    out_ref[at : at + 1, :] = tail[3:4] * node_scale
    out_ref[at + 1 : at + 1 + n, :] = flat[6 * n : 7 * n, :] * node_scale
    out_ref[at + 1 + n : at + 3 + n, :] = tail[4:6] * node_scale


def sum_over_cut(rows, other_work):
    fast = lax.axis_size("cut") // 4
    place = lax.axis_index("cut") // fast
    every = range(4 * fast)

    def ahead(values, k):
        return lax.ppermute(values, "cut", [(i, (i + k * fast) % (4 * fast)) for i in every])

    def across(values, bits):
        return lax.ppermute(values, "cut", [(i, i ^ bits) for i in every])

    def quarter(k):
        return lax.dynamic_index_in_dim(rows, (place + k) % 4, 0, keepdims=False)

    def add(left, right):
        return left.astype(F32) + right.astype(F32)

    first, second, third = [ahead(quarter(k), k) for k in range(1, 4)]
    mine = (add(quarter(0), first) + add(second, third)).astype(BF16)
    terms = [mine] + [across(mine, bits) for bits in range(1, fast)]
    while len(terms) > 1:
        terms = [add(terms[k], terms[k + 1]) for k in range(0, len(terms), 2)]
    mine = terms[0].astype(BF16)
    quarters = [mine] + [ahead(mine, k) for k in range(1, 4)]
    quarters, other_work = lax.optimization_barrier((quarters, other_work))
    return jnp.stack(quarters), place, other_work


VMEM = pl.BlockSpec(memory_space=pltpu.VMEM)
SMEM = pl.BlockSpec(memory_space=pltpu.SMEM)
PARAMS = pltpu.CompilerParams(vmem_limit_bytes=40 * 1024 * 1024)


def whole(kernel, out_shape, n_in, scratch, name, cost=None):
    return pl.pallas_call(
        kernel,
        out_shape=out_shape,
        in_specs=[VMEM] * n_in,
        out_specs=jax.tree.map(lambda _: VMEM, out_shape),
        scratch_shapes=scratch,
        compiler_params=PARAMS,
        interpret=INTERPRET,
        cost_estimate=cost,
        name=name,
    )


def per_device(
    node_feat,
    edge_feat,
    route,
    block_tile,
    block_offset,
    block_count,
    w_edge1,
    bias_edge1,
    w_edge2,
    gain_edge,
    shift_edge,
    w_node1,
    bias_node1,
    w_node2,
    gain_node,
    shift_node,
    node_cot,
):
    latent, masters = node_feat.shape
    slots = edge_feat.shape[1]
    blocks = block_tile.shape[0]
    peers = route.shape[1]
    total_nodes = masters * peers
    total_edges = slots * peers
    tiles = masters // TILE + peers
    shape = jax.ShapeDtypeStruct

    def swap(values):
        return lax.all_to_all(values, "cut", split_axis=0, concat_axis=0, tiled=True)

    def near(values):
        return pltpu.with_memory_space_constraint(values, pltpu.VMEM)

    def hbm(values):
        return pltpu.with_memory_space_constraint(values, pltpu.HBM)

    def sent(dims, dtype):
        return pltpu.HBM(dims, dtype)

    def row(vector):
        return hbm(vector[None, :])

    idx = swap(route[0][:, None, :])
    outgoing = whole(gather_kernel, sent((peers, latent, TILE), BF16), 2, [], "gather")(
        near(idx), hbm(node_feat)
    )
    mirrors = swap(outgoing)

    steps = blocks // GROUP
    width = GROUP * TILE

    def full(dims):
        return pl.BlockSpec(dims, lambda i: (0,) * len(dims))

    def wide(height):
        return pl.BlockSpec((height, width), lambda i: (0, i))

    offsets = pl.BlockSpec((GROUP, 2, TILE), lambda i: (i, 0, 0))
    table = pltpu.VMEM((tiles, latent, TILE), BF16)
    local_sum, sent_back = pl.pallas_call(
        edge_fwd_kernel,
        grid=(steps,),
        out_shape=(sent((latent, masters), F32), sent((peers, latent, TILE), BF16)),
        in_specs=[
            SMEM,
            SMEM,
            offsets,
            wide(latent),
            full((latent, masters)),
            full((peers, latent, TILE)),
            full((latent, 3 * latent)),
            full((1, latent)),
            full((latent, latent)),
            full((1, latent)),
            full((1, latent)),
        ],
        out_specs=(full((latent, masters)), full((peers, latent, TILE))),
        scratch_shapes=[table, pltpu.VMEM((tiles, latent, TILE), F32)],
        compiler_params=PARAMS,
        interpret=INTERPRET,
        name="edge_fwd",
    )(
        hbm(block_tile.T),
        hbm(block_count),
        hbm(block_offset),
        hbm(edge_feat),
        hbm(node_feat),
        near(mirrors),
        hbm(w_edge1),
        row(bias_edge1),
        hbm(w_edge2),
        row(gain_edge),
        row(shift_edge),
    )
    returned = swap(sent_back)
    again, _ = lax.optimization_barrier((mirrors, local_sum))
    pair, hidden, slope, normed, inv = pl.pallas_call(
        edge_keep_kernel,
        grid=(steps,),
        out_shape=(
            sent((2 * latent, slots), BF16),
            sent((latent, slots), BF16),
            sent((latent, slots), F32),
            sent((latent, slots), F32),
            sent((1, slots), F32),
        ),
        in_specs=[
            SMEM,
            offsets,
            wide(latent),
            full((latent, masters)),
            full((peers, latent, TILE)),
            full((latent, 3 * latent)),
            full((1, latent)),
            full((latent, latent)),
        ],
        out_specs=(wide(2 * latent), wide(latent), wide(latent), wide(latent), wide(1)),
        scratch_shapes=[table],
        compiler_params=PARAMS,
        interpret=INTERPRET,
        cost_estimate=pl.CostEstimate(
            flops=12 * latent * latent * slots,
            bytes_accessed=16 * latent * slots,
            transcendentals=latent * slots,
        ),
        name="edge_keep",
    )(
        hbm(block_tile.T),
        hbm(block_offset),
        hbm(edge_feat),
        hbm(node_feat),
        near(again),
        hbm(w_edge1),
        row(bias_edge1),
        hbm(w_edge2),
    )

    agg_low, grad_agg, outgoing = whole(
        node_kernel,
        (
            sent((latent, masters), BF16),
            sent((latent, masters), BF16),
            sent((peers, latent, TILE), BF16),
        ),
        9,
        [],
        "node",
    )(
        near(idx),
        hbm(local_sum),
        near(returned),
        hbm(node_feat),
        hbm(node_cot),
        hbm(w_node1),
        row(bias_node1),
        hbm(w_node2),
        row(gain_node),
    )
    mirrors = swap(outgoing)
    node_out, base, node_rows = whole(
        node_rest_kernel,
        (
            sent((latent, masters), BF16),
            sent((latent, masters), F32),
            sent((3 * latent + 8, TILE), F32),
        ),
        8,
        [],
        "node_rest",
        pl.CostEstimate(
            flops=22 * latent * latent * masters,
            bytes_accessed=20 * latent * masters,
            transcendentals=latent * masters,
        ),
    )(
        hbm(agg_low),
        hbm(node_feat),
        hbm(node_cot),
        hbm(w_node1),
        row(bias_node1),
        hbm(w_node2),
        row(gain_node),
        row(shift_node),
    )

    mirrors = swap(outgoing)

    grad_post, grad_pre, local_grad, returned, sums = pl.pallas_call(
        edge_bwd_kernel,
        grid=(steps,),
        out_shape=(
            sent((latent, slots), BF16),
            sent((latent, slots), BF16),
            sent((latent, masters), F32),
            sent((peers, latent, TILE), BF16),
            sent((3, latent, TILE), F32),
        ),
        in_specs=[
            SMEM,
            SMEM,
            offsets,
            wide(latent),
            wide(latent),
            wide(1),
            full((latent, masters)),
            full((peers, latent, TILE)),
            full((latent, masters)),
            full((latent, 3 * latent)),
            full((latent, latent)),
            full((1, latent)),
        ],
        out_specs=(
            wide(latent),
            wide(latent),
            full((latent, masters)),
            full((peers, latent, TILE)),
            full((3, latent, TILE)),
        ),
        scratch_shapes=[
            pltpu.VMEM((tiles, latent, TILE), BF16),
            pltpu.VMEM((tiles, 2 * latent, TILE), F32),
            pltpu.VMEM((3, latent, TILE), F32),
            pltpu.VMEM((latent, 2 * latent), BF16),
            pltpu.VMEM((latent, latent), BF16),
        ],
        compiler_params=PARAMS,
        interpret=INTERPRET,
        name="edge_bwd",
    )(
        hbm(block_tile.T),
        hbm(block_count),
        hbm(block_offset),
        hbm(slope),
        hbm(normed),
        hbm(inv),
        hbm(grad_agg),
        near(mirrors),
        hbm(base),
        hbm(w_edge1),
        hbm(w_edge2),
        row(gain_edge),
    )
    returned = swap(returned)
    edge_grad, rows = pl.pallas_call(
        edge_weights_kernel,
        grid=(steps,),
        out_shape=(sent((latent, slots), BF16), sent((4 * QUARTER, TILE), BF16)),
        in_specs=[
            wide(latent),
            wide(2 * latent),
            wide(latent),
            wide(latent),
            wide(latent),
            full((latent, 3 * latent)),
            full((3, latent, TILE)),
            full((3 * latent + 8, TILE)),
        ],
        out_specs=(wide(latent), full((4 * QUARTER, TILE))),
        scratch_shapes=[
            pltpu.VMEM((3 * latent, latent), F32),
            pltpu.VMEM((latent, latent), F32),
            pltpu.VMEM((latent, latent), BF16),
        ],
        compiler_params=PARAMS,
        interpret=INTERPRET,
        cost_estimate=pl.CostEstimate(
            flops=10 * latent * latent * slots, bytes_accessed=14 * latent * slots, transcendentals=0
        ),
        name="edge_weights",
    )(
        hbm(edge_feat),
        hbm(pair),
        hbm(hidden),
        hbm(grad_post),
        hbm(grad_pre),
        hbm(w_edge1),
        hbm(sums),
        hbm(node_rows),
    )
    node_grad = whole(final_kernel, sent((latent, masters), F32), 3, [], "final")(
        near(idx), hbm(local_grad), near(returned)
    )
    quarters, place, node_grad = sum_over_cut(rows.reshape(4, QUARTER, TILE), node_grad)
    param_rows = pl.pallas_call(
        functools.partial(
            params_kernel, 1.0 / math.sqrt(total_edges), 1.0 / math.sqrt(total_nodes)
        ),
        out_shape=sent((902, TILE), F32),
        in_specs=[SMEM, VMEM],
        out_specs=VMEM,
        scratch_shapes=[pltpu.VMEM((4 * QUARTER, TILE), F32)],
        compiler_params=PARAMS,
        interpret=INTERPRET,
        name="params",
    )(place.reshape(1), quarters)
    return (node_out, node_grad, edge_grad, param_rows.reshape(-1))


def solution(mesh):
    nodes = P(None, ("dp", "cut"))
    rows = P(("dp", "cut"))
    in_specs = (nodes, nodes, rows, rows, rows, rows) + (P(),) * 10 + (nodes,)
    out_specs = (nodes, nodes, nodes, P("dp"))
    return jax.shard_map(
        per_device, mesh=mesh, in_specs=in_specs, out_specs=out_specs, check_vma=False
    )
```

```python
import functools
import math

import jax
import jax.numpy as jnp
from jax import lax
from jax.experimental import pallas as pl
from jax.experimental.pallas import tpu as pltpu
from jax.sharding import PartitionSpec as P

F32 = jnp.float32
BF16 = jnp.bfloat16
TILE = 128
GROUP = 16
WIDE = 4
QUARTER = 232
INTERPRET = False


def dot_nn(left, right):
    return lax.dot_general(left, right, (((1,), (0,)), ((), ())), preferred_element_type=F32)


def dot_nt(left, right):
    return lax.dot_general(left, right, (((1,), (1,)), ((), ())), preferred_element_type=F32)


def dot_tn(left, right):
    return lax.dot_general(left, right, (((0,), (0,)), ((), ())), preferred_element_type=F32)


def one_hot(index_row, depth):
    rows = lax.broadcasted_iota(jnp.int32, (depth, index_row.shape[1]), 0)
    return jnp.where(rows == index_row, 1.0, 0.0).astype(BF16)


def sigmoid(values):
    return 1.0 / (1.0 + jnp.exp(-values))


def one_hot_rows(index_columns, depth):
    lanes = lax.broadcasted_iota(jnp.int32, (index_columns.shape[0], depth), 1)
    return jnp.where(lanes == index_columns, 1.0, 0.0).astype(BF16)


def column(row_ref):
    return jnp.broadcast_to(row_ref[...], (8, row_ref.shape[1])).T[:, :1]


def layer_norm(values):
    centred = values - jnp.mean(values, axis=0, keepdims=True)
    inverse = lax.rsqrt(jnp.mean(centred * centred, axis=0, keepdims=True) + 1e-05)
    return centred * inverse, inverse


def norm_back(upstream, normed, inverse, gain):
    scaled = upstream * gain
    return inverse * (
        scaled
        - jnp.mean(scaled, axis=0, keepdims=True)
        - normed * jnp.mean(scaled * normed, axis=0, keepdims=True)
    )


def gather_peers(idx_ref, table, store):
    depth = table.shape[1]
    for q in range(0, idx_ref.shape[0], WIDE):
        index_row = jnp.concatenate([idx_ref[q + k] for k in range(WIDE)], axis=1)
        picked = dot_nn(table, one_hot(index_row, depth)).astype(BF16)
        for k in range(WIDE):
            store(q + k, picked[:, k * TILE : (k + 1) * TILE])


def gather_kernel(idx_ref, table_ref, out_ref):
    def store(p, values):
        out_ref[p] = values

    gather_peers(idx_ref, table_ref[...], store)


def fill_table(table, local_ref, mirror_ref):
    local_tiles = local_ref.shape[1] // TILE
    for t in range(local_tiles):
        table[t] = local_ref[:, t * TILE : (t + 1) * TILE]

    def body(p, carry):
        table[local_tiles + p] = mirror_ref[p, :TILE, :]
        return carry

    lax.fori_loop(0, mirror_ref.shape[0], body, 0)


def edge_network(step, tile_ref, offset_ref, edge_ref, table, w1_ref, b1_ref, w2_ref):
    latent = edge_ref.shape[0]
    pairs = []
    for j in range(GROUP):
        b = step * GROUP + j
        both = jnp.concatenate([offset_ref[j, 0:1, :], offset_ref[j, 1:2, :] + TILE], axis=1)
        tiles = jnp.concatenate([table[tile_ref[0, b]], table[tile_ref[1, b]]], axis=1)
        found = dot_nn(tiles, one_hot(both, 2 * TILE)).astype(BF16)
        pairs.append(jnp.concatenate([found[:, :TILE], found[:, TILE:]], axis=0))
    pair = jnp.concatenate(pairs, axis=1)
    pre = (
        dot_nn(w1_ref[:, :latent], edge_ref[...])
        + dot_nn(w1_ref[:, latent:], pair)
        + column(b1_ref)
    )
    gate = sigmoid(pre)
    hidden = (pre * gate).astype(BF16)
    normed, inverse = layer_norm(dot_nn(w2_ref[...], hidden))
    return pair, pre, gate, hidden, normed, inverse


def edge_fwd_kernel(
    tile_ref,
    count_ref,
    offset_ref,
    edge_ref,
    node_ref,
    mirror_ref,
    w1_ref,
    b1_ref,
    w2_ref,
    gain_ref,
    shift_ref,
    local_ref,
    out_ref,
    table,
    total,
):
    step = pl.program_id(0)
    latent = edge_ref.shape[0]
    local_tiles = node_ref.shape[1] // TILE

    @pl.when(step == 0)
    def _():
        fill_table(table, node_ref, mirror_ref)
        total[...] = jnp.zeros_like(total)

    normed = edge_network(step, tile_ref, offset_ref, edge_ref, table, w1_ref, b1_ref, w2_ref)[4]
    message = column(gain_ref) * normed + column(shift_ref)
    turned = offset_ref[:, 1, :].T
    lane = lax.broadcasted_iota(jnp.int32, (latent, TILE), 1)
    spread = []
    for j in range(GROUP):
        values = message[:, j * TILE : (j + 1) * TILE]
        kept = jnp.where(lane < count_ref[step * GROUP + j], values, 0.0).astype(BF16)
        spread.append(dot_nn(kept, one_hot_rows(turned[:, j : j + 1], TILE)))
    for j in range(GROUP):
        total[tile_ref[1, step * GROUP + j]] += spread[j]

    @pl.when(step == pl.num_programs(0) - 1)
    def _():
        for t in range(local_tiles):
            local_ref[:, t * TILE : (t + 1) * TILE] = total[t]

        def body(p, carry):
            out_ref[p] = total[local_tiles + p].astype(BF16)
            return carry

        lax.fori_loop(0, out_ref.shape[0], body, 0)


def edge_keep_kernel(
    tile_ref,
    offset_ref,
    edge_ref,
    node_ref,
    mirror_ref,
    w1_ref,
    b1_ref,
    w2_ref,
    pair_ref,
    hidden_ref,
    slope_ref,
    normed_ref,
    inv_ref,
    table,
):
    step = pl.program_id(0)

    @pl.when(step == 0)
    def _():
        fill_table(table, node_ref, mirror_ref)

    pair, pre, gate, hidden, normed, inverse = edge_network(
        step, tile_ref, offset_ref, edge_ref, table, w1_ref, b1_ref, w2_ref
    )
    pair_ref[...] = pair
    hidden_ref[...] = hidden
    slope_ref[...] = gate * (1.0 + pre * (1.0 - gate))
    normed_ref[...] = normed
    inv_ref[...] = inverse


def scatter_mirrors(total, idx_ref, mirror_ref):
    depth = total.shape[1]
    peers = idx_ref.shape[0]
    turned = jnp.concatenate([idx_ref[p] for p in range(peers)], axis=0).T
    for q in range(0, peers, WIDE):
        hot = jnp.concatenate(
            [one_hot_rows(turned[:, p : p + 1], depth) for p in range(q, q + WIDE)], axis=0
        )
        values = jnp.concatenate([mirror_ref[p, :TILE, :] for p in range(q, q + WIDE)], axis=1)
        total += dot_nn(values, hot)
    return total


def row_sum(values):
    folded = values[:, :TILE]
    for start in range(TILE, values.shape[1], TILE):
        folded = folded + values[:, start : start + TILE]
    return jnp.sum(folded.T, axis=0, keepdims=True)


def node_network(node_low, agg_low, cot_ref, w1_ref, b1_ref, w2_ref, gain):
    latent = node_low.shape[0]
    pre = dot_nn(w1_ref[:, :latent], node_low) + dot_nn(w1_ref[:, latent:], agg_low) + column(b1_ref)
    gate = sigmoid(pre)
    hidden = (pre * gate).astype(BF16)
    normed, inverse = layer_norm(dot_nn(w2_ref[...], hidden))
    upstream = cot_ref[...].astype(F32)
    grad_post = norm_back(upstream, normed, inverse, gain).astype(BF16)
    grad_full = dot_tn(w2_ref[...], grad_post) * (gate * (1.0 + pre * (1.0 - gate)))
    return hidden, normed, upstream, grad_post, grad_full


def node_kernel(
    idx_ref,
    local_ref,
    mirror_ref,
    node_ref,
    cot_ref,
    w1_ref,
    b1_ref,
    w2_ref,
    gain_ref,
    agg_low_ref,
    grad_agg_ref,
    out_ref,
):
    latent = node_ref.shape[0]
    agg_low = scatter_mirrors(local_ref[...], idx_ref, mirror_ref).astype(BF16)
    agg_low_ref[...] = agg_low
    grad_full = node_network(
        node_ref[...], agg_low, cot_ref, w1_ref, b1_ref, w2_ref, column(gain_ref)
    )[4]
    grad_agg = dot_tn(w1_ref[:, latent:], grad_full.astype(BF16)).astype(BF16)
    grad_agg_ref[...] = grad_agg

    def store(p, values):
        out_ref[p] = values

    gather_peers(idx_ref, grad_agg, store)


def node_rest_kernel(
    agg_low_ref,
    node_ref,
    cot_ref,
    w1_ref,
    b1_ref,
    w2_ref,
    gain_ref,
    shift_ref,
    node_out_ref,
    base_ref,
    rows,
):
    latent = node_ref.shape[0]
    node_low, agg_low, gain = node_ref[...], agg_low_ref[...], column(gain_ref)
    hidden, normed, upstream, grad_post, grad_full = node_network(
        node_low, agg_low, cot_ref, w1_ref, b1_ref, w2_ref, gain
    )
    grad_pre = grad_full.astype(BF16)
    node_out_ref[...] = (node_low.astype(F32) + gain * normed + column(shift_ref)).astype(BF16)
    base_ref[...] = upstream + dot_tn(w1_ref[:, :latent], grad_pre)
    rows[0:latent, :] = dot_nt(grad_pre, node_low)
    rows[latent : 2 * latent, :] = dot_nt(grad_pre, agg_low)
    rows[2 * latent : 3 * latent, :] = dot_nt(grad_post, hidden)
    sums = [row_sum(grad_full), row_sum(upstream * normed), row_sum(upstream)]
    rows[3 * latent :, :] = jnp.concatenate(sums + [jnp.zeros((5, TILE), F32)], axis=0)


def edge_bwd_kernel(
    tile_ref,
    count_ref,
    offset_ref,
    slope_ref,
    normed_ref,
    inv_ref,
    agg_ref,
    mirror_ref,
    base_ref,
    w1_ref,
    w2_ref,
    gain_ref,
    post_ref,
    pre_ref,
    local_ref,
    out_ref,
    sums_ref,
    table,
    total,
    sums,
    w1_pair,
    w2_turned,
):
    step = pl.program_id(0)
    latent = slope_ref.shape[0]
    local_tiles = agg_ref.shape[1] // TILE

    @pl.when(step == 0)
    def _():
        fill_table(table, agg_ref, mirror_ref)
        total[...] = jnp.zeros_like(total)
        sums[...] = jnp.zeros_like(sums)
        w2_turned[...] = w2_ref[...].T
        w1_pair[:, :latent] = w1_ref[:, latent : 2 * latent].T
        w1_pair[:, latent:] = w1_ref[:, 2 * latent :].T

    lane = lax.broadcasted_iota(jnp.int32, (latent, TILE), 1)
    gain = column(gain_ref)
    senders = offset_ref[:, 0, :].T
    receivers = offset_ref[:, 1, :].T
    bias_part, gain_part, shift_part = sums[0], sums[1], sums[2]
    picked = []
    for j in range(GROUP):
        b = step * GROUP + j
        found = dot_nn(table[tile_ref[1, b]], one_hot(offset_ref[j, 1:2, :], TILE))
        picked.append(jnp.where(lane < count_ref[b], found, 0.0))
    upstream = jnp.concatenate(picked, axis=1)
    normed = normed_ref[...]
    weighted = upstream * normed
    grad_post = norm_back(upstream, normed, inv_ref[...], gain).astype(BF16)
    post_ref[...] = grad_post
    grad_full = dot_nn(w2_turned[...], grad_post) * slope_ref[...]
    grad_pre = grad_full.astype(BF16)
    pre_ref[...] = grad_pre
    spread = []
    for j in range(GROUP):
        cols = slice(j * TILE, (j + 1) * TILE)
        bias_part += grad_full[:, cols]
        gain_part += weighted[:, cols]
        shift_part += upstream[:, cols]
        hot = jnp.concatenate(
            [
                one_hot_rows(senders[:, j : j + 1], TILE),
                one_hot_rows(receivers[:, j : j + 1], TILE),
            ],
            axis=1,
        )
        spread.append(dot_nn(grad_pre[:, cols], hot))
    for j in range(GROUP):
        b = step * GROUP + j
        total[tile_ref[0, b], :latent, :] += spread[j][:, :TILE]
        total[tile_ref[1, b], latent:, :] += spread[j][:, TILE:]
    sums[0], sums[1], sums[2] = bias_part, gain_part, shift_part

    @pl.when(step == pl.num_programs(0) - 1)
    def _():
        sums_ref[...] = sums[...]
        for t in range(0, table.shape[0], WIDE):
            group = range(t, t + WIDE)
            low = jnp.concatenate([total[k].astype(BF16) for k in group], axis=1)
            back = dot_nn(w1_pair[...], low)
            for k in group:
                part = back[:, (k - t) * TILE : (k - t + 1) * TILE]
                if k < local_tiles:
                    cols = slice(k * TILE, (k + 1) * TILE)
                    local_ref[:, cols] = base_ref[:, cols] + part
                else:
                    out_ref[k - local_tiles] = part.astype(BF16)


def edge_weights_kernel(
    edge_ref,
    pair_ref,
    hidden_ref,
    post_ref,
    pre_ref,
    w1_ref,
    sums_ref,
    node_rows_ref,
    edge_grad_ref,
    rows_ref,
    grad_w1,
    grad_w2,
    w1_turned,
):
    step = pl.program_id(0)
    latent = edge_ref.shape[0]

    @pl.when(step == 0)
    def _():
        grad_w1[...] = jnp.zeros_like(grad_w1)
        grad_w2[...] = jnp.zeros_like(grad_w2)
        w1_turned[...] = w1_ref[:, :latent].T

    grad_pre = pre_ref[...]
    edge_grad_ref[...] = dot_nn(w1_turned[...], grad_pre).astype(BF16)
    grad_w2[...] += dot_nt(post_ref[...], hidden_ref[...])
    grad_w1[:latent] += dot_nt(edge_ref[...], grad_pre)
    grad_w1[latent:] += dot_nt(pair_ref[...], grad_pre)

    @pl.when(step == pl.num_programs(0) - 1)
    def _():
        n = latent
        for c in range(3):
            rows_ref[c * n : (c + 1) * n, :] = grad_w1[c * n : (c + 1) * n, :].T.astype(BF16)
        rows_ref[3 * n : 4 * n, :] = grad_w2[...].astype(BF16)
        rows_ref[4 * n : 7 * n, :] = node_rows_ref[: 3 * n, :].astype(BF16)
        tail = [row_sum(sums_ref[k]) for k in range(3)]
        tail += [node_rows_ref[3 * n : 3 * n + 3, :], jnp.zeros((26, TILE), F32)]
        rows_ref[7 * n :, :] = jnp.concatenate(tail, axis=0).astype(BF16)


def final_kernel(idx_ref, local_ref, mirror_ref, out_ref):
    out_ref[...] = scatter_mirrors(local_ref[...], idx_ref, mirror_ref)


def params_kernel(edge_scale, node_scale, place_ref, quarters_ref, out_ref, flat):
    for q in range(4):
        rows = quarters_ref[(place_ref[0] - q) & 3]
        flat[q * QUARTER : (q + 1) * QUARTER, :] = rows.astype(F32)
    n = TILE
    tail = flat[7 * n : 7 * n + 8, :]
    for c in range(3):
        out_ref[pl.ds(c, n, stride=3), :] = flat[c * n : (c + 1) * n, :] * edge_scale
    out_ref[3 * n : 3 * n + 1, :] = tail[0:1] * edge_scale
    out_ref[3 * n + 1 : 4 * n + 1, :] = flat[3 * n : 4 * n, :] * edge_scale
    out_ref[4 * n + 1 : 4 * n + 3, :] = tail[1:3] * edge_scale
    at = 4 * n + 3
    for c in range(2):
        rows = flat[(4 + c) * n : (5 + c) * n, :]
        out_ref[pl.ds(at + c, n, stride=2), :] = rows * node_scale
    at += 2 * n
    out_ref[at : at + 1, :] = tail[3:4] * node_scale
    out_ref[at + 1 : at + 1 + n, :] = flat[6 * n : 7 * n, :] * node_scale
    out_ref[at + 1 + n : at + 3 + n, :] = tail[4:6] * node_scale


def sum_over_cut(rows, other_work):
    fast = lax.axis_size("cut") // 4
    place = lax.axis_index("cut") // fast
    every = range(4 * fast)

    def ahead(values, k):
        return lax.ppermute(values, "cut", [(i, (i + k * fast) % (4 * fast)) for i in every])

    def across(values, bits):
        return lax.ppermute(values, "cut", [(i, i ^ bits) for i in every])

    def quarter(k):
        return lax.dynamic_index_in_dim(rows, (place + k) % 4, 0, keepdims=False)

    def add(left, right):
        return left.astype(F32) + right.astype(F32)

    first, second, third = [ahead(quarter(k), k) for k in range(1, 4)]
    mine = (add(quarter(0), first) + add(second, third)).astype(BF16)
    one, two = fast // 2, fast // 4
    first, second, third = [across(mine, bits) for bits in (one, two, one | two)]
    mine = (add(mine, first) + add(second, third)).astype(BF16)
    while two > 1:
        two //= 2
        mine = add(mine, across(mine, two)).astype(BF16)
    quarters = [mine] + [ahead(mine, k) for k in range(1, 4)]
    quarters, other_work = lax.optimization_barrier((quarters, other_work))
    return jnp.stack(quarters), place, other_work


VMEM = pl.BlockSpec(memory_space=pltpu.VMEM)
SMEM = pl.BlockSpec(memory_space=pltpu.SMEM)
PARAMS = pltpu.CompilerParams(vmem_limit_bytes=40 * 1024 * 1024)


def whole(kernel, out_shape, n_in, scratch, name, cost=None):
    return pl.pallas_call(
        kernel,
        out_shape=out_shape,
        in_specs=[VMEM] * n_in,
        out_specs=jax.tree.map(lambda _: VMEM, out_shape),
        scratch_shapes=scratch,
        compiler_params=PARAMS,
        interpret=INTERPRET,
        cost_estimate=cost,
        name=name,
    )


def per_device(
    node_feat,
    edge_feat,
    route,
    block_tile,
    block_offset,
    block_count,
    w_edge1,
    bias_edge1,
    w_edge2,
    gain_edge,
    shift_edge,
    w_node1,
    bias_node1,
    w_node2,
    gain_node,
    shift_node,
    node_cot,
):
    latent, masters = node_feat.shape
    slots = edge_feat.shape[1]
    blocks = block_tile.shape[0]
    peers = route.shape[1]
    total_nodes = masters * peers
    total_edges = slots * peers
    tiles = masters // TILE + peers
    shape = jax.ShapeDtypeStruct

    def swap(values):
        return lax.all_to_all(values, "cut", split_axis=0, concat_axis=0, tiled=True)

    def near(values):
        return pltpu.with_memory_space_constraint(values, pltpu.VMEM)

    def hbm(values):
        return pltpu.with_memory_space_constraint(values, pltpu.HBM)

    def sent(dims, dtype):
        return pltpu.HBM(dims, dtype)

    def row(vector):
        return hbm(vector[None, :])

    idx = swap(route[0][:, None, :])
    outgoing = whole(gather_kernel, sent((peers, latent, TILE), BF16), 2, [], "gather")(
        near(idx), hbm(node_feat)
    )
    mirrors = swap(outgoing)

    steps = blocks // GROUP
    width = GROUP * TILE

    def full(dims):
        return pl.BlockSpec(dims, lambda i: (0,) * len(dims))

    def wide(height):
        return pl.BlockSpec((height, width), lambda i: (0, i))

    offsets = pl.BlockSpec((GROUP, 2, TILE), lambda i: (i, 0, 0))
    table = pltpu.VMEM((tiles, latent, TILE), BF16)
    local_sum, sent_back = pl.pallas_call(
        edge_fwd_kernel,
        grid=(steps,),
        out_shape=(sent((latent, masters), F32), sent((peers, latent, TILE), BF16)),
        in_specs=[
            SMEM,
            SMEM,
            offsets,
            wide(latent),
            full((latent, masters)),
            full((peers, latent, TILE)),
            full((latent, 3 * latent)),
            full((1, latent)),
            full((latent, latent)),
            full((1, latent)),
            full((1, latent)),
        ],
        out_specs=(full((latent, masters)), full((peers, latent, TILE))),
        scratch_shapes=[table, pltpu.VMEM((tiles, latent, TILE), F32)],
        compiler_params=PARAMS,
        interpret=INTERPRET,
        name="edge_fwd",
    )(
        hbm(block_tile.T),
        hbm(block_count),
        hbm(block_offset),
        hbm(edge_feat),
        hbm(node_feat),
        near(mirrors),
        hbm(w_edge1),
        row(bias_edge1),
        hbm(w_edge2),
        row(gain_edge),
        row(shift_edge),
    )
    returned = swap(sent_back)
    again, _ = lax.optimization_barrier((mirrors, local_sum))
    pair, hidden, slope, normed, inv = pl.pallas_call(
        edge_keep_kernel,
        grid=(steps,),
        out_shape=(
            sent((2 * latent, slots), BF16),
            sent((latent, slots), BF16),
            sent((latent, slots), F32),
            sent((latent, slots), F32),
            sent((1, slots), F32),
        ),
        in_specs=[
            SMEM,
            offsets,
            wide(latent),
            full((latent, masters)),
            full((peers, latent, TILE)),
            full((latent, 3 * latent)),
            full((1, latent)),
            full((latent, latent)),
        ],
        out_specs=(wide(2 * latent), wide(latent), wide(latent), wide(latent), wide(1)),
        scratch_shapes=[table],
        compiler_params=PARAMS,
        interpret=INTERPRET,
        cost_estimate=pl.CostEstimate(
            flops=12 * latent * latent * slots,
            bytes_accessed=16 * latent * slots,
            transcendentals=latent * slots,
        ),
        name="edge_keep",
    )(
        hbm(block_tile.T),
        hbm(block_offset),
        hbm(edge_feat),
        hbm(node_feat),
        near(again),
        hbm(w_edge1),
        row(bias_edge1),
        hbm(w_edge2),
    )

    agg_low, grad_agg, outgoing = whole(
        node_kernel,
        (
            sent((latent, masters), BF16),
            sent((latent, masters), BF16),
            sent((peers, latent, TILE), BF16),
        ),
        9,
        [],
        "node",
    )(
        near(idx),
        hbm(local_sum),
        near(returned),
        hbm(node_feat),
        hbm(node_cot),
        hbm(w_node1),
        row(bias_node1),
        hbm(w_node2),
        row(gain_node),
    )
    mirrors = swap(outgoing)
    node_out, base, node_rows = whole(
        node_rest_kernel,
        (
            sent((latent, masters), BF16),
            sent((latent, masters), F32),
            sent((3 * latent + 8, TILE), F32),
        ),
        8,
        [],
        "node_rest",
        pl.CostEstimate(
            flops=22 * latent * latent * masters,
            bytes_accessed=20 * latent * masters,
            transcendentals=latent * masters,
        ),
    )(
        hbm(agg_low),
        hbm(node_feat),
        hbm(node_cot),
        hbm(w_node1),
        row(bias_node1),
        hbm(w_node2),
        row(gain_node),
        row(shift_node),
    )

    mirrors = swap(outgoing)

    grad_post, grad_pre, local_grad, returned, sums = pl.pallas_call(
        edge_bwd_kernel,
        grid=(steps,),
        out_shape=(
            sent((latent, slots), BF16),
            sent((latent, slots), BF16),
            sent((latent, masters), F32),
            sent((peers, latent, TILE), BF16),
            sent((3, latent, TILE), F32),
        ),
        in_specs=[
            SMEM,
            SMEM,
            offsets,
            wide(latent),
            wide(latent),
            wide(1),
            full((latent, masters)),
            full((peers, latent, TILE)),
            full((latent, masters)),
            full((latent, 3 * latent)),
            full((latent, latent)),
            full((1, latent)),
        ],
        out_specs=(
            wide(latent),
            wide(latent),
            full((latent, masters)),
            full((peers, latent, TILE)),
            full((3, latent, TILE)),
        ),
        scratch_shapes=[
            pltpu.VMEM((tiles, latent, TILE), BF16),
            pltpu.VMEM((tiles, 2 * latent, TILE), F32),
            pltpu.VMEM((3, latent, TILE), F32),
            pltpu.VMEM((latent, 2 * latent), BF16),
            pltpu.VMEM((latent, latent), BF16),
        ],
        compiler_params=PARAMS,
        interpret=INTERPRET,
        name="edge_bwd",
    )(
        hbm(block_tile.T),
        hbm(block_count),
        hbm(block_offset),
        hbm(slope),
        hbm(normed),
        hbm(inv),
        hbm(grad_agg),
        near(mirrors),
        hbm(base),
        hbm(w_edge1),
        hbm(w_edge2),
        row(gain_edge),
    )
    returned = swap(returned)
    edge_grad, rows = pl.pallas_call(
        edge_weights_kernel,
        grid=(steps,),
        out_shape=(sent((latent, slots), BF16), sent((4 * QUARTER, TILE), BF16)),
        in_specs=[
            wide(latent),
            wide(2 * latent),
            wide(latent),
            wide(latent),
            wide(latent),
            full((latent, 3 * latent)),
            full((3, latent, TILE)),
            full((3 * latent + 8, TILE)),
        ],
        out_specs=(wide(latent), full((4 * QUARTER, TILE))),
        scratch_shapes=[
            pltpu.VMEM((3 * latent, latent), F32),
            pltpu.VMEM((latent, latent), F32),
            pltpu.VMEM((latent, latent), BF16),
        ],
        compiler_params=PARAMS,
        interpret=INTERPRET,
        cost_estimate=pl.CostEstimate(
            flops=10 * latent * latent * slots, bytes_accessed=14 * latent * slots, transcendentals=0
        ),
        name="edge_weights",
    )(
        hbm(edge_feat),
        hbm(pair),
        hbm(hidden),
        hbm(grad_post),
        hbm(grad_pre),
        hbm(w_edge1),
        hbm(sums),
        hbm(node_rows),
    )
    node_grad = whole(final_kernel, sent((latent, masters), F32), 3, [], "final")(
        near(idx), hbm(local_grad), near(returned)
    )
    quarters, place, node_grad = sum_over_cut(rows.reshape(4, QUARTER, TILE), node_grad)
    param_rows = pl.pallas_call(
        functools.partial(
            params_kernel, 1.0 / math.sqrt(total_edges), 1.0 / math.sqrt(total_nodes)
        ),
        out_shape=sent((902, TILE), F32),
        in_specs=[SMEM, VMEM],
        out_specs=VMEM,
        scratch_shapes=[pltpu.VMEM((4 * QUARTER, TILE), F32)],
        compiler_params=PARAMS,
        interpret=INTERPRET,
        name="params",
    )(place.reshape(1), quarters)
    return (node_out, node_grad, edge_grad, param_rows.reshape(-1))


def solution(mesh):
    nodes = P(None, ("dp", "cut"))
    rows = P(("dp", "cut"))
    in_specs = (nodes, nodes, rows, rows, rows, rows) + (P(),) * 10 + (nodes,)
    out_specs = (nodes, nodes, nodes, P("dp"))
    return jax.shard_map(
        per_device, mesh=mesh, in_specs=in_specs, out_specs=out_specs, check_vma=False
    )
```

```python
import functools
import math

import jax
import jax.numpy as jnp
from jax import lax
from jax.experimental import pallas as pl
from jax.experimental.pallas import tpu as pltpu
from jax.sharding import PartitionSpec as P

F32 = jnp.float32
BF16 = jnp.bfloat16
TILE = 128
GROUP = 16
WIDE = 4
QUARTER = 232
INTERPRET = False


def dot_nn(left, right):
    return lax.dot_general(left, right, (((1,), (0,)), ((), ())), preferred_element_type=F32)


def dot_nt(left, right):
    return lax.dot_general(left, right, (((1,), (1,)), ((), ())), preferred_element_type=F32)


def dot_tn(left, right):
    return lax.dot_general(left, right, (((0,), (0,)), ((), ())), preferred_element_type=F32)


def one_hot(index_row, depth):
    rows = lax.broadcasted_iota(jnp.int32, (depth, index_row.shape[1]), 0)
    return jnp.where(rows == index_row, 1.0, 0.0).astype(BF16)


def sigmoid(values):
    return 1.0 / (1.0 + jnp.exp(-values))


def one_hot_rows(index_columns, depth):
    lanes = lax.broadcasted_iota(jnp.int32, (index_columns.shape[0], depth), 1)
    return jnp.where(lanes == index_columns, 1.0, 0.0).astype(BF16)


def column(row_ref):
    return jnp.broadcast_to(row_ref[...], (8, row_ref.shape[1])).T[:, :1]


def layer_norm(values):
    centred = values - jnp.mean(values, axis=0, keepdims=True)
    inverse = lax.rsqrt(jnp.mean(centred * centred, axis=0, keepdims=True) + 1e-05)
    return centred * inverse, inverse


def norm_back(upstream, normed, inverse, gain):
    scaled = upstream * gain
    return inverse * (
        scaled
        - jnp.mean(scaled, axis=0, keepdims=True)
        - normed * jnp.mean(scaled * normed, axis=0, keepdims=True)
    )


def gather_peers(idx_ref, table, store):
    depth = table.shape[1]
    for q in range(0, idx_ref.shape[0], WIDE):
        index_row = jnp.concatenate([idx_ref[q + k] for k in range(WIDE)], axis=1)
        picked = dot_nn(table, one_hot(index_row, depth)).astype(BF16)
        for k in range(WIDE):
            store(q + k, picked[:, k * TILE : (k + 1) * TILE])


def gather_kernel(idx_ref, table_ref, out_ref):
    def store(p, values):
        out_ref[p] = values

    gather_peers(idx_ref, table_ref[...], store)


def fill_table(table, local_ref, mirror_ref):
    local_tiles = local_ref.shape[1] // TILE
    for t in range(local_tiles):
        table[t] = local_ref[:, t * TILE : (t + 1) * TILE]

    for p in range(mirror_ref.shape[0]):
        table[local_tiles + p] = mirror_ref[p]


def edge_network(step, tile_ref, offset_ref, edge_ref, table, w1_ref, b1_ref, w2_ref):
    latent = edge_ref.shape[0]
    pairs = []
    for j in range(GROUP):
        b = step * GROUP + j
        both = jnp.concatenate([offset_ref[j, 0:1, :], offset_ref[j, 1:2, :] + TILE], axis=1)
        tiles = jnp.concatenate([table[tile_ref[0, b]], table[tile_ref[1, b]]], axis=1)
        found = dot_nn(tiles, one_hot(both, 2 * TILE)).astype(BF16)
        pairs.append(jnp.concatenate([found[:, :TILE], found[:, TILE:]], axis=0))
    pair = jnp.concatenate(pairs, axis=1)
    pre = (
        dot_nn(w1_ref[:, :latent], edge_ref[...])
        + dot_nn(w1_ref[:, latent:], pair)
        + column(b1_ref)
    )
    gate = sigmoid(pre)
    hidden = (pre * gate).astype(BF16)
    normed, inverse = layer_norm(dot_nn(w2_ref[...], hidden))
    return pair, pre, gate, hidden, normed, inverse


def edge_fwd_kernel(
    tile_ref,
    count_ref,
    offset_ref,
    edge_ref,
    node_ref,
    mirror_ref,
    w1_ref,
    b1_ref,
    w2_ref,
    gain_ref,
    shift_ref,
    local_ref,
    out_ref,
    table,
    total,
):
    step = pl.program_id(0)
    latent = edge_ref.shape[0]
    local_tiles = node_ref.shape[1] // TILE

    @pl.when(step == 0)
    def _():
        fill_table(table, node_ref, mirror_ref)
        total[...] = jnp.zeros_like(total)

    normed = edge_network(step, tile_ref, offset_ref, edge_ref, table, w1_ref, b1_ref, w2_ref)[4]
    message = column(gain_ref) * normed + column(shift_ref)
    turned = offset_ref[:, 1, :].T
    lane = lax.broadcasted_iota(jnp.int32, (latent, TILE), 1)
    spread = []
    for j in range(GROUP):
        values = message[:, j * TILE : (j + 1) * TILE]
        kept = jnp.where(lane < count_ref[step * GROUP + j], values, 0.0).astype(BF16)
        spread.append(dot_nn(kept, one_hot_rows(turned[:, j : j + 1], TILE)))
    for j in range(GROUP):
        total[tile_ref[1, step * GROUP + j]] += spread[j]

    @pl.when(step == pl.num_programs(0) - 1)
    def _():
        for t in range(local_tiles):
            local_ref[:, t * TILE : (t + 1) * TILE] = total[t]

        for p in range(out_ref.shape[0]):
            out_ref[p] = total[local_tiles + p].astype(BF16)


def edge_keep_kernel(
    tile_ref,
    offset_ref,
    edge_ref,
    node_ref,
    mirror_ref,
    w1_ref,
    b1_ref,
    w2_ref,
    pair_ref,
    hidden_ref,
    slope_ref,
    normed_ref,
    inv_ref,
    table,
):
    step = pl.program_id(0)

    @pl.when(step == 0)
    def _():
        fill_table(table, node_ref, mirror_ref)

    pair, pre, gate, hidden, normed, inverse = edge_network(
        step, tile_ref, offset_ref, edge_ref, table, w1_ref, b1_ref, w2_ref
    )
    pair_ref[...] = pair
    hidden_ref[...] = hidden
    slope_ref[...] = (gate * (1.0 + pre * (1.0 - gate))).astype(BF16)
    normed_ref[...] = normed.astype(BF16)
    inv_ref[...] = inverse


def scatter_mirrors(total, idx_ref, mirror_ref):
    depth = total.shape[1]
    peers = idx_ref.shape[0]
    turned = jnp.concatenate([idx_ref[p] for p in range(peers)], axis=0).T
    for q in range(0, peers, WIDE):
        hot = jnp.concatenate(
            [one_hot_rows(turned[:, p : p + 1], depth) for p in range(q, q + WIDE)], axis=0
        )
        values = jnp.concatenate([mirror_ref[p, :TILE, :] for p in range(q, q + WIDE)], axis=1)
        total += dot_nn(values, hot)
    return total


def row_sum(values):
    folded = values[:, :TILE]
    for start in range(TILE, values.shape[1], TILE):
        folded = folded + values[:, start : start + TILE]
    return jnp.sum(folded.T, axis=0, keepdims=True)


def node_network(node_low, agg_low, cot_ref, w1_ref, b1_ref, w2_ref, gain):
    latent = node_low.shape[0]
    pre = dot_nn(w1_ref[:, :latent], node_low) + dot_nn(w1_ref[:, latent:], agg_low) + column(b1_ref)
    gate = sigmoid(pre)
    hidden = (pre * gate).astype(BF16)
    normed, inverse = layer_norm(dot_nn(w2_ref[...], hidden))
    upstream = cot_ref[...].astype(F32)
    grad_post = norm_back(upstream, normed, inverse, gain).astype(BF16)
    grad_full = dot_tn(w2_ref[...], grad_post) * (gate * (1.0 + pre * (1.0 - gate)))
    return hidden, normed, upstream, grad_post, grad_full


def node_kernel(
    idx_ref,
    local_ref,
    mirror_ref,
    node_ref,
    cot_ref,
    w1_ref,
    b1_ref,
    w2_ref,
    gain_ref,
    agg_low_ref,
    grad_agg_ref,
    out_ref,
):
    latent = node_ref.shape[0]
    agg_low = scatter_mirrors(local_ref[...], idx_ref, mirror_ref).astype(BF16)
    agg_low_ref[...] = agg_low
    grad_full = node_network(
        node_ref[...], agg_low, cot_ref, w1_ref, b1_ref, w2_ref, column(gain_ref)
    )[4]
    grad_agg = dot_tn(w1_ref[:, latent:], grad_full.astype(BF16)).astype(BF16)
    grad_agg_ref[...] = grad_agg

    def store(p, values):
        out_ref[p] = values

    gather_peers(idx_ref, grad_agg, store)


def node_rest_kernel(
    agg_low_ref,
    node_ref,
    cot_ref,
    w1_ref,
    b1_ref,
    w2_ref,
    gain_ref,
    shift_ref,
    node_out_ref,
    base_ref,
    rows,
):
    latent = node_ref.shape[0]
    node_low, agg_low, gain = node_ref[...], agg_low_ref[...], column(gain_ref)
    hidden, normed, upstream, grad_post, grad_full = node_network(
        node_low, agg_low, cot_ref, w1_ref, b1_ref, w2_ref, gain
    )
    grad_pre = grad_full.astype(BF16)
    node_out_ref[...] = (node_low.astype(F32) + gain * normed + column(shift_ref)).astype(BF16)
    base_ref[...] = upstream + dot_tn(w1_ref[:, :latent], grad_pre)
    rows[0:latent, :] = dot_nt(grad_pre, node_low)
    rows[latent : 2 * latent, :] = dot_nt(grad_pre, agg_low)
    rows[2 * latent : 3 * latent, :] = dot_nt(grad_post, hidden)
    sums = [row_sum(grad_full), row_sum(upstream * normed), row_sum(upstream)]
    rows[3 * latent :, :] = jnp.concatenate(sums + [jnp.zeros((5, TILE), F32)], axis=0)


def edge_bwd_kernel(
    tile_ref,
    count_ref,
    offset_ref,
    slope_ref,
    normed_ref,
    inv_ref,
    agg_ref,
    mirror_ref,
    base_ref,
    w1_ref,
    w2_ref,
    gain_ref,
    post_ref,
    pre_ref,
    local_ref,
    out_ref,
    sums_ref,
    table,
    total,
    sums,
    w1_pair,
    w2_turned,
):
    step = pl.program_id(0)
    latent = slope_ref.shape[0]
    local_tiles = agg_ref.shape[1] // TILE

    @pl.when(step == 0)
    def _():
        fill_table(table, agg_ref, mirror_ref)
        total[...] = jnp.zeros_like(total)
        sums[...] = jnp.zeros_like(sums)
        w2_turned[...] = w2_ref[...].T
        w1_pair[:, :latent] = w1_ref[:, latent : 2 * latent].T
        w1_pair[:, latent:] = w1_ref[:, 2 * latent :].T

    lane = lax.broadcasted_iota(jnp.int32, (latent, TILE), 1)
    gain = column(gain_ref)
    senders = offset_ref[:, 0, :].T
    receivers = offset_ref[:, 1, :].T
    bias_part, gain_part, shift_part = sums[0], sums[1], sums[2]
    picked = []
    for j in range(GROUP):
        b = step * GROUP + j
        found = dot_nn(table[tile_ref[1, b]], one_hot(offset_ref[j, 1:2, :], TILE))
        picked.append(jnp.where(lane < count_ref[b], found, 0.0))
    upstream = jnp.concatenate(picked, axis=1)
    normed = normed_ref[...].astype(F32)
    weighted = upstream * normed
    grad_post = norm_back(upstream, normed, inv_ref[...], gain).astype(BF16)
    post_ref[...] = grad_post
    grad_full = dot_nn(w2_turned[...], grad_post) * slope_ref[...]
    grad_pre = grad_full.astype(BF16)
    pre_ref[...] = grad_pre
    spread = []
    for j in range(GROUP):
        cols = slice(j * TILE, (j + 1) * TILE)
        bias_part += grad_full[:, cols]
        gain_part += weighted[:, cols]
        shift_part += upstream[:, cols]
        hot = jnp.concatenate(
            [
                one_hot_rows(senders[:, j : j + 1], TILE),
                one_hot_rows(receivers[:, j : j + 1], TILE),
            ],
            axis=1,
        )
        spread.append(dot_nn(grad_pre[:, cols], hot))
    for j in range(GROUP):
        b = step * GROUP + j
        total[tile_ref[0, b], :latent, :] += spread[j][:, :TILE]
        total[tile_ref[1, b], latent:, :] += spread[j][:, TILE:]
    sums[0], sums[1], sums[2] = bias_part, gain_part, shift_part

    @pl.when(step == pl.num_programs(0) - 1)
    def _():
        sums_ref[...] = sums[...]
        for t in range(0, table.shape[0], WIDE):
            group = range(t, t + WIDE)
            low = jnp.concatenate([total[k].astype(BF16) for k in group], axis=1)
            back = dot_nn(w1_pair[...], low)
            for k in group:
                part = back[:, (k - t) * TILE : (k - t + 1) * TILE]
                if k < local_tiles:
                    cols = slice(k * TILE, (k + 1) * TILE)
                    local_ref[:, cols] = base_ref[:, cols] + part
                else:
                    out_ref[k - local_tiles] = part.astype(BF16)


def edge_weights_kernel(
    edge_ref,
    pair_ref,
    hidden_ref,
    post_ref,
    pre_ref,
    w1_ref,
    sums_ref,
    node_rows_ref,
    edge_grad_ref,
    rows_ref,
    grad_w1,
    grad_w2,
    w1_turned,
):
    step = pl.program_id(0)
    latent = edge_ref.shape[0]

    @pl.when(step == 0)
    def _():
        grad_w1[...] = jnp.zeros_like(grad_w1)
        grad_w2[...] = jnp.zeros_like(grad_w2)
        w1_turned[...] = w1_ref[:, :latent].T

    grad_pre = pre_ref[...]
    edge_grad_ref[...] = dot_nn(w1_turned[...], grad_pre).astype(BF16)
    grad_w2[...] += dot_nt(post_ref[...], hidden_ref[...])
    grad_w1[:latent] += dot_nt(edge_ref[...], grad_pre)
    grad_w1[latent:] += dot_nt(pair_ref[...], grad_pre)

    @pl.when(step == pl.num_programs(0) - 1)
    def _():
        n = latent
        for c in range(3):
            rows_ref[c * n : (c + 1) * n, :] = grad_w1[c * n : (c + 1) * n, :].T.astype(BF16)
        rows_ref[3 * n : 4 * n, :] = grad_w2[...].astype(BF16)
        rows_ref[4 * n : 7 * n, :] = node_rows_ref[: 3 * n, :].astype(BF16)
        tail = [row_sum(sums_ref[k]) for k in range(3)]
        tail += [node_rows_ref[3 * n : 3 * n + 3, :], jnp.zeros((26, TILE), F32)]
        rows_ref[7 * n :, :] = jnp.concatenate(tail, axis=0).astype(BF16)


def final_kernel(idx_ref, local_ref, mirror_ref, out_ref):
    out_ref[...] = scatter_mirrors(local_ref[...], idx_ref, mirror_ref)


def params_kernel(edge_scale, node_scale, place_ref, quarters_ref, out_ref, flat):
    for q in range(4):
        rows = quarters_ref[(place_ref[0] - q) & 3]
        flat[q * QUARTER : (q + 1) * QUARTER, :] = rows.astype(F32)
    n = TILE
    tail = flat[7 * n : 7 * n + 8, :]
    for c in range(3):
        out_ref[pl.ds(c, n, stride=3), :] = flat[c * n : (c + 1) * n, :] * edge_scale
    out_ref[3 * n : 3 * n + 1, :] = tail[0:1] * edge_scale
    out_ref[3 * n + 1 : 4 * n + 1, :] = flat[3 * n : 4 * n, :] * edge_scale
    out_ref[4 * n + 1 : 4 * n + 3, :] = tail[1:3] * edge_scale
    at = 4 * n + 3
    for c in range(2):
        rows = flat[(4 + c) * n : (5 + c) * n, :]
        out_ref[pl.ds(at + c, n, stride=2), :] = rows * node_scale
    at += 2 * n
    out_ref[at : at + 1, :] = tail[3:4] * node_scale
    out_ref[at + 1 : at + 1 + n, :] = flat[6 * n : 7 * n, :] * node_scale
    out_ref[at + 1 + n : at + 3 + n, :] = tail[4:6] * node_scale


def sum_over_cut(rows, other_work):
    fast = lax.axis_size("cut") // 4
    place = lax.axis_index("cut") // fast
    every = range(4 * fast)

    def ahead(values, k):
        return lax.ppermute(values, "cut", [(i, (i + k * fast) % (4 * fast)) for i in every])

    def across(values, bits):
        return lax.ppermute(values, "cut", [(i, i ^ bits) for i in every])

    def quarter(k):
        return lax.dynamic_index_in_dim(rows, (place + k) % 4, 0, keepdims=False)

    def add(left, right):
        return left.astype(F32) + right.astype(F32)

    first, second, third = [ahead(quarter(k), k) for k in range(1, 4)]
    mine = (add(quarter(0), first) + add(second, third)).astype(BF16)
    one, two = fast // 2, fast // 4
    first, second, third = [across(mine, bits) for bits in (one, two, one | two)]
    mine = (add(mine, first) + add(second, third)).astype(BF16)
    while two > 1:
        two //= 2
        mine = add(mine, across(mine, two)).astype(BF16)
    quarters = [mine] + [ahead(mine, k) for k in range(1, 4)]
    quarters, other_work = lax.optimization_barrier((quarters, other_work))
    return jnp.stack(quarters), place, other_work


VMEM = pl.BlockSpec(memory_space=pltpu.VMEM)
SMEM = pl.BlockSpec(memory_space=pltpu.SMEM)
PARAMS = pltpu.CompilerParams(vmem_limit_bytes=40 * 1024 * 1024)


def whole(kernel, out_shape, n_in, scratch, name, cost=None):
    return pl.pallas_call(
        kernel,
        out_shape=out_shape,
        in_specs=[VMEM] * n_in,
        out_specs=jax.tree.map(lambda _: VMEM, out_shape),
        scratch_shapes=scratch,
        compiler_params=PARAMS,
        interpret=INTERPRET,
        cost_estimate=cost,
        name=name,
    )


def per_device(
    node_feat,
    edge_feat,
    route,
    block_tile,
    block_offset,
    block_count,
    w_edge1,
    bias_edge1,
    w_edge2,
    gain_edge,
    shift_edge,
    w_node1,
    bias_node1,
    w_node2,
    gain_node,
    shift_node,
    node_cot,
):
    latent, masters = node_feat.shape
    slots = edge_feat.shape[1]
    blocks = block_tile.shape[0]
    peers = route.shape[1]
    total_nodes = masters * peers
    total_edges = slots * peers
    tiles = masters // TILE + peers
    shape = jax.ShapeDtypeStruct

    def swap(values):
        return lax.all_to_all(values, "cut", split_axis=0, concat_axis=0, tiled=True)

    def near(values):
        return pltpu.with_memory_space_constraint(values, pltpu.VMEM)

    def hbm(values):
        return pltpu.with_memory_space_constraint(values, pltpu.HBM)

    def sent(dims, dtype):
        return pltpu.HBM(dims, dtype)

    def row(vector):
        return hbm(vector[None, :])

    idx = swap(route[0][:, None, :])
    outgoing = whole(gather_kernel, sent((peers, latent, TILE), BF16), 2, [], "gather")(
        near(idx), hbm(node_feat)
    )
    mirrors = swap(outgoing)

    steps = blocks // GROUP
    width = GROUP * TILE

    def full(dims):
        return pl.BlockSpec(dims, lambda i: (0,) * len(dims))

    def wide(height):
        return pl.BlockSpec((height, width), lambda i: (0, i))

    offsets = pl.BlockSpec((GROUP, 2, TILE), lambda i: (i, 0, 0))
    table = pltpu.VMEM((tiles, latent, TILE), BF16)
    local_sum, sent_back = pl.pallas_call(
        edge_fwd_kernel,
        grid=(steps,),
        out_shape=(sent((latent, masters), F32), sent((peers, latent, TILE), BF16)),
        in_specs=[
            SMEM,
            SMEM,
            offsets,
            wide(latent),
            full((latent, masters)),
            full((peers, latent, TILE)),
            full((latent, 3 * latent)),
            full((1, latent)),
            full((latent, latent)),
            full((1, latent)),
            full((1, latent)),
        ],
        out_specs=(full((latent, masters)), full((peers, latent, TILE))),
        scratch_shapes=[table, pltpu.VMEM((tiles, latent, TILE), F32)],
        compiler_params=PARAMS,
        interpret=INTERPRET,
        name="edge_fwd",
    )(
        hbm(block_tile.T),
        hbm(block_count),
        hbm(block_offset),
        hbm(edge_feat),
        hbm(node_feat),
        near(mirrors),
        hbm(w_edge1),
        row(bias_edge1),
        hbm(w_edge2),
        row(gain_edge),
        row(shift_edge),
    )
    returned = swap(sent_back)
    again, _ = lax.optimization_barrier((mirrors, local_sum))
    pair, hidden, slope, normed, inv = pl.pallas_call(
        edge_keep_kernel,
        grid=(steps,),
        out_shape=(
            sent((2 * latent, slots), BF16),
            sent((latent, slots), BF16),
            sent((latent, slots), BF16),
            sent((latent, slots), BF16),
            sent((1, slots), F32),
        ),
        in_specs=[
            SMEM,
            offsets,
            wide(latent),
            full((latent, masters)),
            full((peers, latent, TILE)),
            full((latent, 3 * latent)),
            full((1, latent)),
            full((latent, latent)),
        ],
        out_specs=(wide(2 * latent), wide(latent), wide(latent), wide(latent), wide(1)),
        scratch_shapes=[table],
        compiler_params=PARAMS,
        interpret=INTERPRET,
        cost_estimate=pl.CostEstimate(
            flops=12 * latent * latent * slots,
            bytes_accessed=16 * latent * slots,
            transcendentals=latent * slots,
        ),
        name="edge_keep",
    )(
        hbm(block_tile.T),
        hbm(block_offset),
        hbm(edge_feat),
        hbm(node_feat),
        near(again),
        hbm(w_edge1),
        row(bias_edge1),
        hbm(w_edge2),
    )

    agg_low, grad_agg, outgoing = whole(
        node_kernel,
        (
            sent((latent, masters), BF16),
            sent((latent, masters), BF16),
            sent((peers, latent, TILE), BF16),
        ),
        9,
        [],
        "node",
    )(
        near(idx),
        hbm(local_sum),
        near(returned),
        hbm(node_feat),
        hbm(node_cot),
        hbm(w_node1),
        row(bias_node1),
        hbm(w_node2),
        row(gain_node),
    )
    mirrors = swap(outgoing)
    node_out, base, node_rows = whole(
        node_rest_kernel,
        (
            sent((latent, masters), BF16),
            sent((latent, masters), F32),
            sent((3 * latent + 8, TILE), F32),
        ),
        8,
        [],
        "node_rest",
        pl.CostEstimate(
            flops=22 * latent * latent * masters,
            bytes_accessed=20 * latent * masters,
            transcendentals=latent * masters,
        ),
    )(
        hbm(agg_low),
        hbm(node_feat),
        hbm(node_cot),
        hbm(w_node1),
        row(bias_node1),
        hbm(w_node2),
        row(gain_node),
        row(shift_node),
    )

    mirrors = swap(outgoing)

    grad_post, grad_pre, local_grad, returned, sums = pl.pallas_call(
        edge_bwd_kernel,
        grid=(steps,),
        out_shape=(
            sent((latent, slots), BF16),
            sent((latent, slots), BF16),
            sent((latent, masters), F32),
            sent((peers, latent, TILE), BF16),
            sent((3, latent, TILE), F32),
        ),
        in_specs=[
            SMEM,
            SMEM,
            offsets,
            wide(latent),
            wide(latent),
            wide(1),
            full((latent, masters)),
            full((peers, latent, TILE)),
            full((latent, masters)),
            full((latent, 3 * latent)),
            full((latent, latent)),
            full((1, latent)),
        ],
        out_specs=(
            wide(latent),
            wide(latent),
            full((latent, masters)),
            full((peers, latent, TILE)),
            full((3, latent, TILE)),
        ),
        scratch_shapes=[
            pltpu.VMEM((tiles, latent, TILE), BF16),
            pltpu.VMEM((tiles, 2 * latent, TILE), F32),
            pltpu.VMEM((3, latent, TILE), F32),
            pltpu.VMEM((latent, 2 * latent), BF16),
            pltpu.VMEM((latent, latent), BF16),
        ],
        compiler_params=PARAMS,
        interpret=INTERPRET,
        name="edge_bwd",
    )(
        hbm(block_tile.T),
        hbm(block_count),
        hbm(block_offset),
        hbm(slope),
        hbm(normed),
        hbm(inv),
        hbm(grad_agg),
        near(mirrors),
        hbm(base),
        hbm(w_edge1),
        hbm(w_edge2),
        row(gain_edge),
    )
    returned = swap(returned)
    edge_grad, rows = pl.pallas_call(
        edge_weights_kernel,
        grid=(steps,),
        out_shape=(sent((latent, slots), BF16), sent((4 * QUARTER, TILE), BF16)),
        in_specs=[
            wide(latent),
            wide(2 * latent),
            wide(latent),
            wide(latent),
            wide(latent),
            full((latent, 3 * latent)),
            full((3, latent, TILE)),
            full((3 * latent + 8, TILE)),
        ],
        out_specs=(wide(latent), full((4 * QUARTER, TILE))),
        scratch_shapes=[
            pltpu.VMEM((3 * latent, latent), F32),
            pltpu.VMEM((latent, latent), F32),
            pltpu.VMEM((latent, latent), BF16),
        ],
        compiler_params=PARAMS,
        interpret=INTERPRET,
        cost_estimate=pl.CostEstimate(
            flops=10 * latent * latent * slots, bytes_accessed=14 * latent * slots, transcendentals=0
        ),
        name="edge_weights",
    )(
        hbm(edge_feat),
        hbm(pair),
        hbm(hidden),
        hbm(grad_post),
        hbm(grad_pre),
        hbm(w_edge1),
        hbm(sums),
        hbm(node_rows),
    )
    node_grad = whole(final_kernel, sent((latent, masters), F32), 3, [], "final")(
        near(idx), hbm(local_grad), near(returned)
    )
    quarters, place, node_grad = sum_over_cut(rows.reshape(4, QUARTER, TILE), node_grad)
    param_rows = pl.pallas_call(
        functools.partial(
            params_kernel, 1.0 / math.sqrt(total_edges), 1.0 / math.sqrt(total_nodes)
        ),
        out_shape=sent((902, TILE), F32),
        in_specs=[SMEM, VMEM],
        out_specs=VMEM,
        scratch_shapes=[pltpu.VMEM((4 * QUARTER, TILE), F32)],
        compiler_params=PARAMS,
        interpret=INTERPRET,
        name="params",
    )(place.reshape(1), quarters)
    return (node_out, node_grad, edge_grad, param_rows.reshape(-1))


def solution(mesh):
    nodes = P(None, ("dp", "cut"))
    rows = P(("dp", "cut"))
    in_specs = (nodes, nodes, rows, rows, rows, rows) + (P(),) * 10 + (nodes,)
    out_specs = (nodes, nodes, nodes, P("dp"))
    return jax.shard_map(
        per_device, mesh=mesh, in_specs=in_specs, out_specs=out_specs, check_vma=False
    )
```

```python
import functools
import math

import jax
import jax.numpy as jnp
from jax import lax
from jax.experimental import pallas as pl
from jax.experimental.pallas import tpu as pltpu
from jax.sharding import PartitionSpec as P

F32 = jnp.float32
BF16 = jnp.bfloat16
TILE = 128
GROUP = 16
WIDE = 8
QUARTER = 232
INTERPRET = False


def dot_nn(left, right):
    return lax.dot_general(left, right, (((1,), (0,)), ((), ())), preferred_element_type=F32)


def dot_nt(left, right):
    return lax.dot_general(left, right, (((1,), (1,)), ((), ())), preferred_element_type=F32)


def dot_tn(left, right):
    return lax.dot_general(left, right, (((0,), (0,)), ((), ())), preferred_element_type=F32)


def one_hot(index_row, depth):
    rows = lax.broadcasted_iota(jnp.int32, (depth, index_row.shape[1]), 0)
    return jnp.where(rows == index_row, 1.0, 0.0).astype(BF16)


def sigmoid(values):
    return 1.0 / (1.0 + jnp.exp(-values))


def one_hot_rows(index_columns, depth):
    lanes = lax.broadcasted_iota(jnp.int32, (index_columns.shape[0], depth), 1)
    return jnp.where(lanes == index_columns, 1.0, 0.0).astype(BF16)


def column(row_ref):
    return jnp.broadcast_to(row_ref[...], (8, row_ref.shape[1])).T[:, :1]


def layer_norm(values):
    centred = values - jnp.mean(values, axis=0, keepdims=True)
    inverse = lax.rsqrt(jnp.mean(centred * centred, axis=0, keepdims=True) + 1e-05)
    return centred * inverse, inverse


def norm_back(upstream, normed, inverse, gain):
    scaled = upstream * gain
    return inverse * (
        scaled
        - jnp.mean(scaled, axis=0, keepdims=True)
        - normed * jnp.mean(scaled * normed, axis=0, keepdims=True)
    )


def gather_peers(idx_ref, table, store):
    depth = table.shape[1]
    for q in range(0, idx_ref.shape[0], WIDE):
        index_row = jnp.concatenate([idx_ref[q + k] for k in range(WIDE)], axis=1)
        picked = dot_nn(table, one_hot(index_row, depth)).astype(BF16)
        for k in range(WIDE):
            store(q + k, picked[:, k * TILE : (k + 1) * TILE])


def gather_kernel(idx_ref, table_ref, out_ref):
    def store(p, values):
        out_ref[p] = values

    gather_peers(idx_ref, table_ref[...], store)


def fill_table(table, local_ref, mirror_ref):
    local_tiles = local_ref.shape[1] // TILE
    for t in range(local_tiles):
        table[t] = local_ref[:, t * TILE : (t + 1) * TILE]

    for p in range(mirror_ref.shape[0]):
        table[local_tiles + p] = mirror_ref[p]


def edge_network(step, tile_ref, offset_ref, edge_ref, table, w1_ref, b1_ref, w2_ref):
    latent = edge_ref.shape[0]
    pairs = []
    for j in range(GROUP):
        b = step * GROUP + j
        both = jnp.concatenate([offset_ref[j, 0:1, :], offset_ref[j, 1:2, :] + TILE], axis=1)
        tiles = jnp.concatenate([table[tile_ref[0, b]], table[tile_ref[1, b]]], axis=1)
        found = dot_nn(tiles, one_hot(both, 2 * TILE)).astype(BF16)
        pairs.append(jnp.concatenate([found[:, :TILE], found[:, TILE:]], axis=0))
    pair = jnp.concatenate(pairs, axis=1)
    pre = (
        dot_nn(w1_ref[:, :latent], edge_ref[...])
        + dot_nn(w1_ref[:, latent:], pair)
        + column(b1_ref)
    )
    gate = sigmoid(pre)
    hidden = (pre * gate).astype(BF16)
    normed, inverse = layer_norm(dot_nn(w2_ref[...], hidden))
    return pair, pre, gate, hidden, normed, inverse


def edge_fwd_kernel(
    tile_ref,
    count_ref,
    offset_ref,
    edge_ref,
    node_ref,
    mirror_ref,
    w1_ref,
    b1_ref,
    w2_ref,
    gain_ref,
    shift_ref,
    local_ref,
    out_ref,
    table,
    total,
):
    step = pl.program_id(0)
    latent = edge_ref.shape[0]
    local_tiles = node_ref.shape[1] // TILE

    @pl.when(step == 0)
    def _():
        fill_table(table, node_ref, mirror_ref)
        total[...] = jnp.zeros_like(total)

    normed = edge_network(step, tile_ref, offset_ref, edge_ref, table, w1_ref, b1_ref, w2_ref)[4]
    message = column(gain_ref) * normed + column(shift_ref)
    turned = offset_ref[:, 1, :].T
    lane = lax.broadcasted_iota(jnp.int32, (latent, TILE), 1)
    spread = []
    for j in range(GROUP):
        values = message[:, j * TILE : (j + 1) * TILE]
        kept = jnp.where(lane < count_ref[step * GROUP + j], values, 0.0).astype(BF16)
        spread.append(dot_nn(kept, one_hot_rows(turned[:, j : j + 1], TILE)))
    for j in range(GROUP):
        total[tile_ref[1, step * GROUP + j]] += spread[j]

    @pl.when(step == pl.num_programs(0) - 1)
    def _():
        for t in range(local_tiles):
            local_ref[:, t * TILE : (t + 1) * TILE] = total[t]

        for p in range(out_ref.shape[0]):
            out_ref[p] = total[local_tiles + p].astype(BF16)


def edge_keep_kernel(
    tile_ref,
    offset_ref,
    edge_ref,
    node_ref,
    mirror_ref,
    w1_ref,
    b1_ref,
    w2_ref,
    pair_ref,
    hidden_ref,
    slope_ref,
    normed_ref,
    inv_ref,
    table,
):
    step = pl.program_id(0)

    @pl.when(step == 0)
    def _():
        fill_table(table, node_ref, mirror_ref)

    pair, pre, gate, hidden, normed, inverse = edge_network(
        step, tile_ref, offset_ref, edge_ref, table, w1_ref, b1_ref, w2_ref
    )
    pair_ref[...] = pair
    hidden_ref[...] = hidden
    slope_ref[...] = (gate * (1.0 + pre * (1.0 - gate))).astype(BF16)
    normed_ref[...] = normed.astype(BF16)
    inv_ref[...] = inverse


def scatter_mirrors(total, idx_ref, mirror_ref):
    depth = total.shape[1]
    peers = idx_ref.shape[0]
    turned = jnp.concatenate([idx_ref[p] for p in range(peers)], axis=0).T
    for q in range(0, peers, WIDE):
        hot = jnp.concatenate(
            [one_hot_rows(turned[:, p : p + 1], depth) for p in range(q, q + WIDE)], axis=0
        )
        values = jnp.concatenate([mirror_ref[p, :TILE, :] for p in range(q, q + WIDE)], axis=1)
        total += dot_nn(values, hot)
    return total


def row_sum(values):
    folded = values[:, :TILE]
    for start in range(TILE, values.shape[1], TILE):
        folded = folded + values[:, start : start + TILE]
    return jnp.sum(folded.T, axis=0, keepdims=True)


def node_network(node_low, agg_low, cot_ref, w1_ref, b1_ref, w2_ref, gain):
    latent = node_low.shape[0]
    pre = dot_nn(w1_ref[:, :latent], node_low) + dot_nn(w1_ref[:, latent:], agg_low) + column(b1_ref)
    gate = sigmoid(pre)
    hidden = (pre * gate).astype(BF16)
    normed, inverse = layer_norm(dot_nn(w2_ref[...], hidden))
    upstream = cot_ref[...].astype(F32)
    grad_post = norm_back(upstream, normed, inverse, gain).astype(BF16)
    grad_full = dot_tn(w2_ref[...], grad_post) * (gate * (1.0 + pre * (1.0 - gate)))
    return hidden, normed, upstream, grad_post, grad_full


def node_kernel(
    idx_ref,
    local_ref,
    mirror_ref,
    node_ref,
    cot_ref,
    w1_ref,
    b1_ref,
    w2_ref,
    gain_ref,
    agg_low_ref,
    grad_agg_ref,
    out_ref,
):
    latent = node_ref.shape[0]
    agg_low = scatter_mirrors(local_ref[...], idx_ref, mirror_ref).astype(BF16)
    agg_low_ref[...] = agg_low
    grad_full = node_network(
        node_ref[...], agg_low, cot_ref, w1_ref, b1_ref, w2_ref, column(gain_ref)
    )[4]
    grad_agg = dot_tn(w1_ref[:, latent:], grad_full.astype(BF16)).astype(BF16)
    grad_agg_ref[...] = grad_agg

    def store(p, values):
        out_ref[p] = values

    gather_peers(idx_ref, grad_agg, store)


def node_rest_kernel(
    agg_low_ref,
    node_ref,
    cot_ref,
    w1_ref,
    b1_ref,
    w2_ref,
    gain_ref,
    shift_ref,
    node_out_ref,
    base_ref,
    rows,
):
    latent = node_ref.shape[0]
    node_low, agg_low, gain = node_ref[...], agg_low_ref[...], column(gain_ref)
    hidden, normed, upstream, grad_post, grad_full = node_network(
        node_low, agg_low, cot_ref, w1_ref, b1_ref, w2_ref, gain
    )
    grad_pre = grad_full.astype(BF16)
    node_out_ref[...] = (node_low.astype(F32) + gain * normed + column(shift_ref)).astype(BF16)
    base_ref[...] = upstream + dot_tn(w1_ref[:, :latent], grad_pre)
    rows[0:latent, :] = dot_nt(grad_pre, node_low)
    rows[latent : 2 * latent, :] = dot_nt(grad_pre, agg_low)
    rows[2 * latent : 3 * latent, :] = dot_nt(grad_post, hidden)
    sums = [row_sum(grad_full), row_sum(upstream * normed), row_sum(upstream)]
    rows[3 * latent :, :] = jnp.concatenate(sums + [jnp.zeros((5, TILE), F32)], axis=0)


def edge_bwd_kernel(
    tile_ref,
    count_ref,
    offset_ref,
    slope_ref,
    normed_ref,
    inv_ref,
    agg_ref,
    mirror_ref,
    base_ref,
    w1_ref,
    w2_ref,
    gain_ref,
    post_ref,
    pre_ref,
    local_ref,
    out_ref,
    sums_ref,
    table,
    total,
    sums,
    w1_pair,
    w2_turned,
):
    step = pl.program_id(0)
    latent = slope_ref.shape[0]
    local_tiles = agg_ref.shape[1] // TILE

    @pl.when(step == 0)
    def _():
        fill_table(table, agg_ref, mirror_ref)
        total[...] = jnp.zeros_like(total)
        sums[...] = jnp.zeros_like(sums)
        w2_turned[...] = w2_ref[...].T
        w1_pair[:, :latent] = w1_ref[:, latent : 2 * latent].T
        w1_pair[:, latent:] = w1_ref[:, 2 * latent :].T

    lane = lax.broadcasted_iota(jnp.int32, (latent, TILE), 1)
    gain = column(gain_ref)
    senders = offset_ref[:, 0, :].T
    receivers = offset_ref[:, 1, :].T
    bias_part, gain_part, shift_part = sums[0], sums[1], sums[2]
    picked = []
    for j in range(GROUP):
        b = step * GROUP + j
        found = dot_nn(table[tile_ref[1, b]], one_hot(offset_ref[j, 1:2, :], TILE))
        picked.append(jnp.where(lane < count_ref[b], found, 0.0))
    upstream = jnp.concatenate(picked, axis=1)
    normed = normed_ref[...].astype(F32)
    weighted = upstream * normed
    grad_post = norm_back(upstream, normed, inv_ref[...], gain).astype(BF16)
    post_ref[...] = grad_post
    grad_full = dot_nn(w2_turned[...], grad_post) * slope_ref[...]
    grad_pre = grad_full.astype(BF16)
    pre_ref[...] = grad_pre
    spread = []
    for j in range(GROUP):
        cols = slice(j * TILE, (j + 1) * TILE)
        bias_part += grad_full[:, cols]
        gain_part += weighted[:, cols]
        shift_part += upstream[:, cols]
        hot = jnp.concatenate(
            [
                one_hot_rows(senders[:, j : j + 1], TILE),
                one_hot_rows(receivers[:, j : j + 1], TILE),
            ],
            axis=1,
        )
        spread.append(dot_nn(grad_pre[:, cols], hot))
    for j in range(GROUP):
        b = step * GROUP + j
        total[tile_ref[0, b], :latent, :] += spread[j][:, :TILE]
        total[tile_ref[1, b], latent:, :] += spread[j][:, TILE:]
    sums[0], sums[1], sums[2] = bias_part, gain_part, shift_part

    @pl.when(step == pl.num_programs(0) - 1)
    def _():
        sums_ref[...] = sums[...]
        for t in range(0, table.shape[0], WIDE):
            group = range(t, t + WIDE)
            low = jnp.concatenate([total[k].astype(BF16) for k in group], axis=1)
            back = dot_nn(w1_pair[...], low)
            for k in group:
                part = back[:, (k - t) * TILE : (k - t + 1) * TILE]
                if k < local_tiles:
                    cols = slice(k * TILE, (k + 1) * TILE)
                    local_ref[:, cols] = base_ref[:, cols] + part
                else:
                    out_ref[k - local_tiles] = part.astype(BF16)


def edge_weights_kernel(
    edge_ref,
    pair_ref,
    hidden_ref,
    post_ref,
    pre_ref,
    w1_ref,
    sums_ref,
    node_rows_ref,
    edge_grad_ref,
    rows_ref,
    grad_w1,
    grad_w2,
    w1_turned,
):
    step = pl.program_id(0)
    latent = edge_ref.shape[0]

    @pl.when(step == 0)
    def _():
        grad_w1[...] = jnp.zeros_like(grad_w1)
        grad_w2[...] = jnp.zeros_like(grad_w2)
        w1_turned[...] = w1_ref[:, :latent].T

    grad_pre = pre_ref[...]
    edge_grad_ref[...] = dot_nn(w1_turned[...], grad_pre).astype(BF16)
    grad_w2[...] += dot_nt(post_ref[...], hidden_ref[...])
    grad_w1[:latent] += dot_nt(edge_ref[...], grad_pre)
    grad_w1[latent:] += dot_nt(pair_ref[...], grad_pre)

    @pl.when(step == pl.num_programs(0) - 1)
    def _():
        n = latent
        for c in range(3):
            rows_ref[c * n : (c + 1) * n, :] = grad_w1[c * n : (c + 1) * n, :].T.astype(BF16)
        rows_ref[3 * n : 4 * n, :] = grad_w2[...].astype(BF16)
        rows_ref[4 * n : 7 * n, :] = node_rows_ref[: 3 * n, :].astype(BF16)
        tail = [row_sum(sums_ref[k]) for k in range(3)]
        tail += [node_rows_ref[3 * n : 3 * n + 3, :], jnp.zeros((26, TILE), F32)]
        rows_ref[7 * n :, :] = jnp.concatenate(tail, axis=0).astype(BF16)


def final_kernel(idx_ref, local_ref, mirror_ref, out_ref):
    out_ref[...] = scatter_mirrors(local_ref[...], idx_ref, mirror_ref)


def params_kernel(edge_scale, node_scale, place_ref, quarters_ref, out_ref, flat):
    for q in range(4):
        rows = quarters_ref[(place_ref[0] - q) & 3]
        flat[q * QUARTER : (q + 1) * QUARTER, :] = rows.astype(F32)
    n = TILE
    tail = flat[7 * n : 7 * n + 8, :]
    for c in range(3):
        out_ref[pl.ds(c, n, stride=3), :] = flat[c * n : (c + 1) * n, :] * edge_scale
    out_ref[3 * n : 3 * n + 1, :] = tail[0:1] * edge_scale
    out_ref[3 * n + 1 : 4 * n + 1, :] = flat[3 * n : 4 * n, :] * edge_scale
    out_ref[4 * n + 1 : 4 * n + 3, :] = tail[1:3] * edge_scale
    at = 4 * n + 3
    for c in range(2):
        rows = flat[(4 + c) * n : (5 + c) * n, :]
        out_ref[pl.ds(at + c, n, stride=2), :] = rows * node_scale
    at += 2 * n
    out_ref[at : at + 1, :] = tail[3:4] * node_scale
    out_ref[at + 1 : at + 1 + n, :] = flat[6 * n : 7 * n, :] * node_scale
    out_ref[at + 1 + n : at + 3 + n, :] = tail[4:6] * node_scale


def sum_over_cut(rows, other_work):
    fast = lax.axis_size("cut") // 4
    place = lax.axis_index("cut") // fast
    every = range(4 * fast)

    def ahead(values, k):
        return lax.ppermute(values, "cut", [(i, (i + k * fast) % (4 * fast)) for i in every])

    def across(values, bits):
        return lax.ppermute(values, "cut", [(i, i ^ bits) for i in every])

    def quarter(k):
        return lax.dynamic_index_in_dim(rows, (place + k) % 4, 0, keepdims=False)

    def add(left, right):
        return left.astype(F32) + right.astype(F32)

    first, second, third = [ahead(quarter(k), k) for k in range(1, 4)]
    mine = (add(quarter(0), first) + add(second, third)).astype(BF16)
    one, two = fast // 2, fast // 4
    first, second, third = [across(mine, bits) for bits in (one, two, one | two)]
    mine = (add(mine, first) + add(second, third)).astype(BF16)
    while two > 1:
        two //= 2
        mine = add(mine, across(mine, two)).astype(BF16)
    quarters = [mine] + [ahead(mine, k) for k in range(1, 4)]
    quarters, other_work = lax.optimization_barrier((quarters, other_work))
    return jnp.stack(quarters), place, other_work


VMEM = pl.BlockSpec(memory_space=pltpu.VMEM)
SMEM = pl.BlockSpec(memory_space=pltpu.SMEM)
PARAMS = pltpu.CompilerParams(vmem_limit_bytes=40 * 1024 * 1024)


def whole(kernel, out_shape, n_in, scratch, name, cost=None):
    return pl.pallas_call(
        kernel,
        out_shape=out_shape,
        in_specs=[VMEM] * n_in,
        out_specs=jax.tree.map(lambda _: VMEM, out_shape),
        scratch_shapes=scratch,
        compiler_params=PARAMS,
        interpret=INTERPRET,
        cost_estimate=cost,
        name=name,
    )


def per_device(
    node_feat,
    edge_feat,
    route,
    block_tile,
    block_offset,
    block_count,
    w_edge1,
    bias_edge1,
    w_edge2,
    gain_edge,
    shift_edge,
    w_node1,
    bias_node1,
    w_node2,
    gain_node,
    shift_node,
    node_cot,
):
    latent, masters = node_feat.shape
    slots = edge_feat.shape[1]
    blocks = block_tile.shape[0]
    peers = route.shape[1]
    total_nodes = masters * peers
    total_edges = slots * peers
    tiles = masters // TILE + peers
    shape = jax.ShapeDtypeStruct

    def swap(values):
        return lax.all_to_all(values, "cut", split_axis=0, concat_axis=0, tiled=True)

    def near(values):
        return pltpu.with_memory_space_constraint(values, pltpu.VMEM)

    def hbm(values):
        return pltpu.with_memory_space_constraint(values, pltpu.HBM)

    def sent(dims, dtype):
        return pltpu.HBM(dims, dtype)

    def row(vector):
        return hbm(vector[None, :])

    idx = swap(route[0][:, None, :])
    outgoing = whole(gather_kernel, sent((peers, latent, TILE), BF16), 2, [], "gather")(
        near(idx), hbm(node_feat)
    )
    mirrors = swap(outgoing)

    steps = blocks // GROUP
    width = GROUP * TILE

    def full(dims):
        return pl.BlockSpec(dims, lambda i: (0,) * len(dims))

    def wide(height):
        return pl.BlockSpec((height, width), lambda i: (0, i))

    offsets = pl.BlockSpec((GROUP, 2, TILE), lambda i: (i, 0, 0))
    table = pltpu.VMEM((tiles, latent, TILE), BF16)
    local_sum, sent_back = pl.pallas_call(
        edge_fwd_kernel,
        grid=(steps,),
        out_shape=(sent((latent, masters), F32), sent((peers, latent, TILE), BF16)),
        in_specs=[
            SMEM,
            SMEM,
            offsets,
            wide(latent),
            full((latent, masters)),
            full((peers, latent, TILE)),
            full((latent, 3 * latent)),
            full((1, latent)),
            full((latent, latent)),
            full((1, latent)),
            full((1, latent)),
        ],
        out_specs=(full((latent, masters)), full((peers, latent, TILE))),
        scratch_shapes=[table, pltpu.VMEM((tiles, latent, TILE), F32)],
        compiler_params=PARAMS,
        interpret=INTERPRET,
        name="edge_fwd",
    )(
        hbm(block_tile.T),
        hbm(block_count),
        hbm(block_offset),
        hbm(edge_feat),
        hbm(node_feat),
        near(mirrors),
        hbm(w_edge1),
        row(bias_edge1),
        hbm(w_edge2),
        row(gain_edge),
        row(shift_edge),
    )
    returned = swap(sent_back)
    again, _ = lax.optimization_barrier((mirrors, local_sum))
    pair, hidden, slope, normed, inv = pl.pallas_call(
        edge_keep_kernel,
        grid=(steps,),
        out_shape=(
            sent((2 * latent, slots), BF16),
            sent((latent, slots), BF16),
            sent((latent, slots), BF16),
            sent((latent, slots), BF16),
            sent((1, slots), F32),
        ),
        in_specs=[
            SMEM,
            offsets,
            wide(latent),
            full((latent, masters)),
            full((peers, latent, TILE)),
            full((latent, 3 * latent)),
            full((1, latent)),
            full((latent, latent)),
        ],
        out_specs=(wide(2 * latent), wide(latent), wide(latent), wide(latent), wide(1)),
        scratch_shapes=[table],
        compiler_params=PARAMS,
        interpret=INTERPRET,
        cost_estimate=pl.CostEstimate(
            flops=12 * latent * latent * slots,
            bytes_accessed=16 * latent * slots,
            transcendentals=latent * slots,
        ),
        name="edge_keep",
    )(
        hbm(block_tile.T),
        hbm(block_offset),
        hbm(edge_feat),
        hbm(node_feat),
        near(again),
        hbm(w_edge1),
        row(bias_edge1),
        hbm(w_edge2),
    )

    agg_low, grad_agg, outgoing = whole(
        node_kernel,
        (
            sent((latent, masters), BF16),
            sent((latent, masters), BF16),
            sent((peers, latent, TILE), BF16),
        ),
        9,
        [],
        "node",
    )(
        near(idx),
        hbm(local_sum),
        near(returned),
        hbm(node_feat),
        hbm(node_cot),
        hbm(w_node1),
        row(bias_node1),
        hbm(w_node2),
        row(gain_node),
    )
    mirrors = swap(outgoing)
    node_out, base, node_rows = whole(
        node_rest_kernel,
        (
            sent((latent, masters), BF16),
            sent((latent, masters), F32),
            sent((3 * latent + 8, TILE), F32),
        ),
        8,
        [],
        "node_rest",
        pl.CostEstimate(
            flops=22 * latent * latent * masters,
            bytes_accessed=20 * latent * masters,
            transcendentals=latent * masters,
        ),
    )(
        hbm(agg_low),
        hbm(node_feat),
        hbm(node_cot),
        hbm(w_node1),
        row(bias_node1),
        hbm(w_node2),
        row(gain_node),
        row(shift_node),
    )

    mirrors = swap(outgoing)

    grad_post, grad_pre, local_grad, returned, sums = pl.pallas_call(
        edge_bwd_kernel,
        grid=(steps,),
        out_shape=(
            sent((latent, slots), BF16),
            sent((latent, slots), BF16),
            sent((latent, masters), F32),
            sent((peers, latent, TILE), BF16),
            sent((3, latent, TILE), F32),
        ),
        in_specs=[
            SMEM,
            SMEM,
            offsets,
            wide(latent),
            wide(latent),
            wide(1),
            full((latent, masters)),
            full((peers, latent, TILE)),
            full((latent, masters)),
            full((latent, 3 * latent)),
            full((latent, latent)),
            full((1, latent)),
        ],
        out_specs=(
            wide(latent),
            wide(latent),
            full((latent, masters)),
            full((peers, latent, TILE)),
            full((3, latent, TILE)),
        ),
        scratch_shapes=[
            pltpu.VMEM((tiles, latent, TILE), BF16),
            pltpu.VMEM((tiles, 2 * latent, TILE), F32),
            pltpu.VMEM((3, latent, TILE), F32),
            pltpu.VMEM((latent, 2 * latent), BF16),
            pltpu.VMEM((latent, latent), BF16),
        ],
        compiler_params=PARAMS,
        interpret=INTERPRET,
        name="edge_bwd",
    )(
        hbm(block_tile.T),
        hbm(block_count),
        hbm(block_offset),
        hbm(slope),
        hbm(normed),
        hbm(inv),
        hbm(grad_agg),
        near(mirrors),
        hbm(base),
        hbm(w_edge1),
        hbm(w_edge2),
        row(gain_edge),
    )
    returned = swap(returned)
    edge_grad, rows = pl.pallas_call(
        edge_weights_kernel,
        grid=(steps,),
        out_shape=(sent((latent, slots), BF16), sent((4 * QUARTER, TILE), BF16)),
        in_specs=[
            wide(latent),
            wide(2 * latent),
            wide(latent),
            wide(latent),
            wide(latent),
            full((latent, 3 * latent)),
            full((3, latent, TILE)),
            full((3 * latent + 8, TILE)),
        ],
        out_specs=(wide(latent), full((4 * QUARTER, TILE))),
        scratch_shapes=[
            pltpu.VMEM((3 * latent, latent), F32),
            pltpu.VMEM((latent, latent), F32),
            pltpu.VMEM((latent, latent), BF16),
        ],
        compiler_params=PARAMS,
        interpret=INTERPRET,
        cost_estimate=pl.CostEstimate(
            flops=10 * latent * latent * slots, bytes_accessed=14 * latent * slots, transcendentals=0
        ),
        name="edge_weights",
    )(
        hbm(edge_feat),
        hbm(pair),
        hbm(hidden),
        hbm(grad_post),
        hbm(grad_pre),
        hbm(w_edge1),
        hbm(sums),
        hbm(node_rows),
    )
    node_grad = whole(final_kernel, sent((latent, masters), F32), 3, [], "final")(
        near(idx), hbm(local_grad), near(returned)
    )
    quarters, place, node_grad = sum_over_cut(rows.reshape(4, QUARTER, TILE), node_grad)
    param_rows = pl.pallas_call(
        functools.partial(
            params_kernel, 1.0 / math.sqrt(total_edges), 1.0 / math.sqrt(total_nodes)
        ),
        out_shape=sent((902, TILE), F32),
        in_specs=[SMEM, VMEM],
        out_specs=VMEM,
        scratch_shapes=[pltpu.VMEM((4 * QUARTER, TILE), F32)],
        compiler_params=PARAMS,
        interpret=INTERPRET,
        name="params",
    )(place.reshape(1), quarters)
    return (node_out, node_grad, edge_grad, param_rows.reshape(-1))


def solution(mesh):
    nodes = P(None, ("dp", "cut"))
    rows = P(("dp", "cut"))
    in_specs = (nodes, nodes, rows, rows, rows, rows) + (P(),) * 10 + (nodes,)
    out_specs = (nodes, nodes, nodes, P("dp"))
    return jax.shard_map(
        per_device, mesh=mesh, in_specs=in_specs, out_specs=out_specs, check_vma=False
    )
```
